32 devices in a mesh: gx: 8 (over z, y), gy: 2 (over core), gz: 2 (over x).
Axes of the slice: x: 2, y: 2, z: 4, core: 2. Of those that a mesh axis runs over, the one named last changes fastest.
Arguments:
- conserved: bfloat16 [5, 64, 16, 256], P(None, 'gx', 'gy', 'gz'), may hold values from -0.5 to 5, as said below
- sigma_prev: float32 [64, 16, 256], P('gx', 'gy', 'gz'), may hold values from -6 to 6
Outputs:
- new_state: float32 [5, 64, 16, 256], P(None, 'gx', 'gy', 'gz')
- entropic: float32 [64, 16, 256], P('gx', 'gy', 'gz')
The draws below stay inside these ranges and needn't reach their ends.
Inputs may be any that keep to these rules, and one draw needn't show every extreme that they name: `conserved`: field 0 (density) lies in 0.5 to 2, fields 1 to 3 (momenta) in -0.5 to 0.5, field 4 (total energy) in 2 to 5.
All inputs are finite; a program needn't handle non-finite values.
Results may differ from the reference program's by a relative error of at most 0.0013.
Values may be sent and summed in bfloat16 or wider, within the bound.
A program may use at most 64 MiB of HBM per device.

```python
import jax
import jax.numpy as jnp
from jax import lax

SWEEPS = 4
NX = 64
NY = 16
NZ = 256


def draw_conserved(key, part):
    subkeys = jax.random.split(jax.random.fold_in(key, 17), 3)
    grid_shape = (NX, NY, NZ)
    rough_density = jax.random.uniform(subkeys[0], grid_shape, jnp.float32)
    rough_energy = jax.random.uniform(subkeys[2], grid_shape, jnp.float32)
    momentum = jax.random.uniform(subkeys[1], (3,) + grid_shape, jnp.float32, -0.5, 0.5)
    density = 0.5 + 1.5 * rough_density
    energy = 2.0 + 3.0 * rough_energy
    stacked = jnp.concatenate([density[None], momentum, energy[None]], axis=0)
    return stacked.astype(jnp.bfloat16)


def level_of(rng, shape, cuts, low, largest):
    gain, own = 1.0, jax.random.fold_in(rng, 6)
    for dim, parts in cuts:
        draws = jnp.exp(jax.random.uniform(jax.random.fold_in(own, dim), (parts,), jnp.float32, low / len(cuts), largest / len(cuts)))
        gain = gain * jnp.repeat(draws, shape[dim] // parts).reshape([-1 if axis == dim else 1 for axis in range(len(shape))])
    return gain


def centred(stream_key, extent, width, most, pieces=(), kind=jnp.bfloat16):
    drawn = jax.random.normal(stream_key, extent, jnp.float32) * width
    if len(pieces) > 0:
        drawn = level_of(stream_key, extent, pieces, -0.22, 0.18) * drawn
    return jnp.clip(drawn, min=-most, max=most).astype(kind)


def setup_inputs(seed: int = 0) -> dict:
    arg_keys = jax.random.split(jax.random.key(seed), 3)
    conserved = draw_conserved(jax.random.fold_in(arg_keys[2], 71), 0)
    sigma_prev = centred(arg_keys[1], (NX, NY, NZ), 1.0, 6.0, ((0, 8), (1, 2), (2, 2)), jnp.float32)
    return {"conserved": conserved, "sigma_prev": sigma_prev}


gamma_gas = 1.4
alpha_reg = 4.0
time_step = 0.08

def crop(tensor, margin):
    return tensor[..., margin:tensor.shape[-3] - margin, margin:tensor.shape[-2] - margin, margin:tensor.shape[-1] - margin]

def cut_axis(tensor, axis_dim, start, length):
    return lax.slice_in_dim(tensor, start, start + length, axis=axis_dim)

def trim_except(tensor, keep_axis, margin):
    for spatial in range(3):
        if spatial != keep_axis:
            axis_dim = tensor.ndim - 3 + spatial
            tensor = cut_axis(tensor, axis_dim, margin, tensor.shape[axis_dim] - 2 * margin)
    return tensor

def central(tensor, spatial):
    axis_dim = tensor.ndim - 3 + spatial
    length = tensor.shape[axis_dim] - 2
    return 0.5 * (cut_axis(tensor, axis_dim, 2, length) - cut_axis(tensor, axis_dim, 0, length))

def stencil(padded):
    center = padded[1:-1, 1:-1, 1:-1]
    beside_all = [padded[2:, 1:-1, 1:-1], padded[:-2, 1:-1, 1:-1], padded[1:-1, 2:, 1:-1], padded[1:-1, :-2, 1:-1], padded[1:-1, 1:-1, 2:], padded[1:-1, 1:-1, :-2]]
    return (center, beside_all)

def sweep(sigma_pad, inverse_pad, source):
    sigma_mid, sigma_around = stencil(sigma_pad)
    inverse_mid, inverse_around = stencil(inverse_pad)
    numerator = source
    denominator = inverse_mid
    for neighbor_sigma, neighbor_inverse in zip(sigma_around, inverse_around):
        weight = alpha_reg * 0.5 * (inverse_mid + neighbor_inverse)
        numerator = numerator + weight * neighbor_sigma
        denominator = denominator + weight
    return numerator / denominator

def entropic_source(halo_state, margin):
    region = crop(halo_state, 2 - margin)
    velocity = region[1:4] / region[0]
    gradient = [trim_except(central(velocity, spatial), spatial, 1) for spatial in range(3)]
    divergence = gradient[0][0] + gradient[1][1] + gradient[2][2]
    product = divergence * divergence
    for first in range(3):
        for second in range(3):
            product = product + gradient[first][second] * gradient[second][first]
    return alpha_reg * product

def physical_flux(values, spatial):
    density = values[0]
    velocity = values[1:4] / density
    kinetic = 0.5 * (values[1] * velocity[0] + values[2] * velocity[1] + values[3] * velocity[2])
    pressure = (gamma_gas - 1.0) * (values[4] - kinetic)
    normal = velocity[spatial]
    momentum = [values[1 + component] * normal for component in range(3)]
    momentum[spatial] = momentum[spatial] + pressure
    flux_vec = jnp.stack([values[1 + spatial]] + momentum + [(values[4] + pressure) * normal])
    wave_speed = jnp.abs(normal) + jnp.sqrt(gamma_gas * jnp.abs(pressure) / density)
    return (flux_vec, wave_speed)

def flux_divergence(halo_state, sigma_pad):
    summed = None
    for spatial in range(3):
        pencil = trim_except(halo_state, spatial, 3)
        axis_dim = spatial + 1
        face_count = pencil.shape[axis_dim] - 5
        shifted = [cut_axis(pencil, axis_dim, offset, face_count) for offset in range(6)]
        left_state = (2.0 * shifted[0] - 13.0 * shifted[1] + 47.0 * shifted[2] + 27.0 * shifted[3] - 3.0 * shifted[4]) / 60.0
        right_state = (2.0 * shifted[5] - 13.0 * shifted[4] + 47.0 * shifted[3] + 27.0 * shifted[2] - 3.0 * shifted[1]) / 60.0
        flux_left, speed_left = physical_flux(left_state, spatial)
        flux_right, speed_right = physical_flux(right_state, spatial)
        numeric = 0.5 * (flux_left + flux_right) - 0.5 * jnp.maximum(speed_left, speed_right) * (right_state - left_state)
        change = cut_axis(numeric, axis_dim, 1, face_count - 1) - cut_axis(numeric, axis_dim, 0, face_count - 1)
        sigma_line = trim_except(sigma_pad, spatial, 1)
        grad_sigma = central(sigma_line, spatial)
        vel_line = cut_axis(pencil, axis_dim, 2, face_count + 1)
        vel_normal = vel_line[1 + spatial] / vel_line[0]
        power_term = central(sigma_line * vel_normal, spatial)
        update = [change[index] for index in range(5)]
        update[1 + spatial] = update[1 + spatial] + grad_sigma
        update[4] = update[4] + power_term
        increment = jnp.stack(update)
        summed = increment if summed is None else summed + increment
    return -summed

def wrap_pad(tensor, depth_cells):
    widths = [(0, 0)] * (tensor.ndim - 3) + [(depth_cells, depth_cells)] * 3
    return jnp.pad(tensor, widths, mode='wrap')

def reference(conserved, sigma_prev):
    initial = conserved.astype(jnp.float32)
    section_state = conserved
    entropic = sigma_prev
    new_state = initial
    for section_index in range(2):
        halo_state = wrap_pad(section_state, 3).astype(jnp.float32)
        source = entropic_source(halo_state, 0)
        inverse = crop(1.0 / halo_state[0], 2)
        for sweep_index in range(SWEEPS):
            entropic = sweep(wrap_pad(entropic, 1), inverse, source)
        tendency = flux_divergence(halo_state, wrap_pad(entropic, 1))
        if section_index == 0:
            section_state = (initial + time_step * tendency).astype(jnp.bfloat16)
        else:
            new_state = 0.5 * (initial + section_state.astype(jnp.float32) + time_step * tendency)
    return (new_state, entropic)
```

```python
import functools

import jax
import jax.numpy as jnp
from jax import lax
from jax.experimental import pallas as pl
from jax.experimental.pallas import tpu as pltpu
from jax.sharding import PartitionSpec as P

SWEEPS = 4
HALO = SWEEPS + 1
REACH = 3
gamma_gas = 1.4
alpha_reg = 4.0
time_step = 0.08
MESH = pl.DeviceIdType.MESH
F32 = jnp.float32
BF16 = jnp.bfloat16


def edges(c, p1, m1, p2, m2):
    even = (47.0 / 60.0) * c + (7.0 / 60.0) * (p1 + m1) - (0.5 / 60.0) * (p2 + m2)
    odd = (20.0 / 60.0) * (p1 - m1) - (2.5 / 60.0) * (p2 - m2)
    return even + odd, even - odd


def physical_flux(v, d):
    inv = 1.0 / v[0]
    u = [v[1] * inv, v[2] * inv, v[3] * inv]
    kinetic = 0.5 * (v[1] * u[0] + v[2] * u[1] + v[3] * u[2])
    p = (gamma_gas - 1.0) * (v[4] - kinetic)
    n = u[d]
    flux = [v[1 + d], v[1] * n, v[2] * n, v[3] * n, (v[4] + p) * n]
    flux[1 + d] = flux[1 + d] + p
    return flux, jnp.abs(n) + jnp.sqrt(gamma_gas * jnp.abs(p) * inv)


def face_flux(left, right, d):
    fl, sl = physical_flux(left, d)
    fr, sr = physical_flux(right, d)
    speed = jnp.maximum(sl, sr)
    return [0.5 * ((a + b) - speed * (r - l)) for a, b, l, r in zip(fl, fr, left, right)]


def up(v, axis, by=1):
    return pltpu.roll(v, (v.shape[axis] - by) % v.shape[axis], axis)


def down(v, axis, by=1):
    return pltpu.roll(v, by, axis)


def kernel(counts, cons, sigma, new_out, ent_out, xq, xe, xs, yq, ys, yxq, yxs, pq, ps, rq, rs,
           st1, sg1, QF, U, INV, CO, SA, SB, T, send_sem, recv_sem):
    gx, gy, gz = lax.axis_index("gx"), lax.axis_index("gy"), lax.axis_index("gz")
    nx, ny, nz = sigma.shape
    px = nx + 2 * HALO
    slot = nz // nx
    own_y, own_z = slice(0, ny), slice(0, nz)
    far_y, far_z = slice(ny, 2 * ny), slice(nz, 2 * nz)

    def dev(dx, dy, dz):
        return (
            lax.rem(gx + dx + counts[0], counts[0]),
            lax.rem(gy + dy, counts[1]),
            lax.rem(gz + dz, counts[2]),
        )

    lane = lax.broadcasted_iota(jnp.int32, (ny, nz), 1)

    def pack(sec, q, s):
        for f in range(6):
            acc = None
            for k in range(nx):
                v = q[f, k].astype(F32) if f < 5 else s[k]
                r = pltpu.roll(v, (HALO + slot * k) % nz, 1)
                acc = r if acc is None else jnp.where(lane >= slot * k, r, acc)
            if f < 5:
                pq[sec, f] = acc.astype(BF16)
            else:
                ps[sec] = acc

    peers = [(-1, 0, 0), (1, 0, 0), (0, 1, 0)] + [
        (dx, dy, 1) for dx in (0, -1, 1) for dy in (0, 1)
    ]

    def section(sec, q, s):
        number = [0]

        def copy(src, dst, where):
            k = number[0]
            number[0] += 1
            return pltpu.make_async_remote_copy(
                src_ref=src, dst_ref=dst, send_sem=send_sem.at[sec, k],
                recv_sem=recv_sem.at[sec, k], device_id=dev(*where), device_id_type=MESH,
            )

        x_copies = []
        for side in (0, 1):
            to = (1, 0, 0) if side == 0 else (-1, 0, 0)
            a = nx - HALO if side == 0 else 0
            b = nx - REACH if side == 0 else 0
            x_copies.append([
                copy(q.at[0:4, a:a + HALO], xq.at[sec, side], to),
                copy(s.at[a:a + HALO], xs.at[sec, side], to),
                copy(q.at[4, b:b + REACH], xe.at[sec, side], to),
            ])
        y_copies = [copy(q, yq.at[sec], (0, 1, 0)), copy(s, ys.at[sec], (0, 1, 0))]
        relays = [
            [copy(xq.at[sec, side], yxq.at[sec, side], (0, 1, 0)),
             copy(xs.at[sec, side], yxs.at[sec, side], (0, 1, 0))]
            for side in (0, 1)
        ]
        z_copies = {}
        for dx, dy, dz in peers[3:]:
            z_copies[(1 - dx, dy)] = [
                copy(pq.at[sec], rq.at[sec, 1 - dx, dy], (dx, dy, dz)),
                copy(ps.at[sec], rs.at[sec, 1 - dx, dy], (dx, dy, dz)),
            ]
        everything = x_copies[0] + x_copies[1] + y_copies + relays[0] + relays[1]
        for both in z_copies.values():
            everything = everything + both

        for pair in x_copies:
            for c in pair:
                c.start()
        for c in y_copies:
            c.start()
        if sec == 1:
            pack(sec, q, s)
        for both in z_copies.values():
            for c in both:
                c.start()

        for k in range(nx):
            for f in range(5):
                QF[f, HALO + k, own_y, own_z] = q[f, k].astype(F32)
            SA[HALO + k, own_y, own_z] = s[k]

        def unpack(j, dy, k, plane, fields):
            rows = far_y if dy else own_y
            back = (nz - (HALO + slot * k) % nz) % nz
            for f in range(fields):
                QF[f, plane, rows, far_z] = pltpu.roll(rq[sec, j, dy, f].astype(F32), back, 1)
            SA[plane, rows, far_z] = pltpu.roll(rs[sec, j, dy], back, 1)

        for c in y_copies:
            c.wait_recv()
        for k in range(nx):
            for f in range(5):
                QF[f, HALO + k, far_y, own_z] = yq[sec, f, k].astype(F32)
            SA[HALO + k, far_y, own_z] = ys[sec, k]
        for dy in (0, 1):
            for c in z_copies[(1, dy)]:
                c.wait_recv()
            for k in range(nx):
                unpack(1, dy, k, HALO + k, 5)

        def side_flux(k, carry):
            p = HALO + k
            total = None
            for d, axis, rows, cols in ((1, 0, slice(0, 2 * ny), own_z), (2, 1, own_y, slice(0, 2 * nz))):
                left, right = [], []
                for f in range(5):
                    c = QF[f, p, rows, cols]
                    l, r = edges(c, up(c, axis), down(c, axis), up(c, axis, 2), down(c, axis, 2))
                    left.append(l)
                    right.append(up(r, axis))
                h = face_flux(left, right, d)
                change = [(v - down(v, axis))[own_y, own_z] for v in h]
                total = change if total is None else [a + b for a, b in zip(total, change)]
            for f in range(5):
                T[f, k] = total[f]
            return carry

        lax.fori_loop(0, nx, side_flux, 0)

        for side in (0, 1):
            for c in x_copies[side]:
                c.wait_recv()
            for c in relays[side]:
                c.start()
        for side in (0, 1):
            base = 0 if side == 0 else HALO + nx
            ebase = HALO - REACH if side == 0 else HALO + nx
            for k in range(HALO):
                for f in range(4):
                    QF[f, base + k, own_y, own_z] = xq[sec, side, f, k].astype(F32)
                SA[base + k, own_y, own_z] = xs[sec, side, k]
            for k in range(REACH):
                QF[4, ebase + k, own_y, own_z] = xe[sec, side, k].astype(F32)

        def x_face(p):
            left, right = [], []
            for f in range(5):
                v = [QF[f, p + o, own_y, own_z] for o in range(-2, 4)]
                left.append(edges(v[2], v[3], v[1], v[4], v[0])[0])
                right.append(edges(v[3], v[4], v[2], v[5], v[1])[1])
            return face_flux(left, right, 0)

        def x_flux(k, before):
            h = x_face(HALO + k)
            for f in range(5):
                T[f, k] = T[f, k] + (h[f] - before[f])
            return tuple(h)

        lax.fori_loop(0, nx, x_flux, tuple(x_face(HALO - 1)), unroll=2)

        for side in (0, 1):
            j = 0 if side == 0 else 2
            base = 0 if side == 0 else HALO + nx
            first = nx - HALO if side == 0 else 0
            for dy in (0, 1):
                for c in z_copies[(j, dy)]:
                    c.wait_recv()
                for k in range(HALO):
                    unpack(j, dy, first + k, base + k, 4)
        for side in (0, 1):
            base = 0 if side == 0 else HALO + nx
            for c in relays[side]:
                c.wait_recv()
            for k in range(HALO):
                for f in range(4):
                    QF[f, base + k, far_y, own_z] = yxq[sec, side, f, k].astype(F32)
                SA[base + k, far_y, own_z] = yxs[sec, side, k]

        def velocities(p, carry):
            inv = 1.0 / QF[0, p]
            INV[p] = inv
            for a in range(3):
                U[a, p] = QF[1 + a, p] * inv
            return carry

        lax.fori_loop(0, px, velocities, 0, unroll=2)

        def coefficients(p, carry):
            g = []
            for a in range(3):
                u = U[a, p]
                g.append([
                    U[a, p + 1] - U[a, p - 1], up(u, 0) - down(u, 0), up(u, 1) - down(u, 1),
                ])
            div = g[0][0] + g[1][1] + g[2][2]
            total = div * div + g[0][0] * g[0][0] + g[1][1] * g[1][1] + g[2][2] * g[2][2]
            total = total + 2.0 * (g[0][1] * g[1][0] + g[0][2] * g[2][0] + g[1][2] * g[2][1])
            source = (alpha_reg * 0.25) * total
            c = INV[p]
            around = [INV[p + 1], INV[p - 1], up(c, 0), down(c, 0), up(c, 1), down(c, 1)]
            w = [(alpha_reg * 0.5) * (c + n) for n in around]
            scale = 1.0 / (c + ((w[0] + w[1]) + (w[2] + w[3]) + (w[4] + w[5])))
            for n in range(6):
                CO[n, p] = w[n] * scale
            CO[6, p] = source * scale
            return carry

        lax.fori_loop(1, px - 1, coefficients, 0)

        read, write = SA, SB
        for step in range(SWEEPS):
            def one(p, carry, read=read, write=write):
                c = read[p]
                out = CO[6, p] + CO[0, p] * read[p + 1] + CO[1, p] * read[p - 1]
                out = out + (CO[2, p] * up(c, 0) + CO[3, p] * down(c, 0))
                out = out + (CO[4, p] * up(c, 1) + CO[5, p] * down(c, 1))
                write[p] = out
                return carry

            lax.fori_loop(step + 1, px - 1 - step, one, 0, unroll=2)
            read, write = write, read
        S = read

        def finish(k, carry):
            p = HALO + k
            tile = (own_y, own_z)
            push = [T[f, k] for f in range(5)]
            xp, xm = S[(p + 1,) + tile], S[(p - 1,) + tile]
            push[1] = push[1] + 0.5 * (xp - xm)
            power = xp * U[(0, p + 1) + tile] - xm * U[(0, p - 1) + tile]
            sy = S[p, :, own_z]
            push[2] = push[2] + 0.5 * (up(sy, 0) - down(sy, 0))[own_y, own_z]
            e = sy * U[1, p, :, own_z]
            power = power + (up(e, 0) - down(e, 0))[own_y, own_z]
            sz = S[p, own_y, :]
            push[3] = push[3] + 0.5 * (up(sz, 1) - down(sz, 1))[own_y, own_z]
            e = sz * U[2, p, own_y, :]
            power = power + (up(e, 1) - down(e, 1))[own_y, own_z]
            push[4] = push[4] + 0.5 * power
            for f in range(5):
                initial = cons[f, k].astype(F32)
                moved = initial - time_step * push[f]
                if sec == 0:
                    st1[f, k] = moved.astype(BF16)
                else:
                    new_out[f, k] = 0.5 * (moved + st1[f, k].astype(F32))
            mid = S[(p,) + tile]
            if sec == 0:
                sg1[k] = mid
            else:
                ent_out[k] = mid
            return carry

        lax.fori_loop(0, nx, finish, 0, unroll=2)
        return everything

    pack(0, cons, sigma)
    barrier = pltpu.get_barrier_semaphore()
    for peer in peers:
        pl.semaphore_signal(barrier, inc=1, device_id=dev(*peer), device_id_type=MESH)
    pl.semaphore_wait(barrier, len(peers))
    first = section(0, cons, sigma)
    second = section(1, st1, sg1)
    for c in first + second:
        c.wait_send()


def solution(mesh):
    counts = (mesh.shape["gx"], mesh.shape["gy"], mesh.shape["gz"])
    assert counts[1] == 2 and counts[2] == 2

    def step(conserved, sigma_prev):
        _, nx, ny, nz = conserved.shape
        px = nx + 2 * HALO
        wide = (2 * ny, 2 * nz)
        vmem = pl.BlockSpec(memory_space=pltpu.VMEM)
        return pl.pallas_call(
            functools.partial(kernel, counts),
            out_shape=(
                jax.ShapeDtypeStruct((5, nx, ny, nz), F32),
                jax.ShapeDtypeStruct((nx, ny, nz), F32),
            ),
            in_specs=[vmem, vmem],
            out_specs=(vmem, vmem),
            scratch_shapes=[
                pltpu.VMEM((2, 2, 4, HALO, ny, nz), BF16),
                pltpu.VMEM((2, 2, REACH, ny, nz), BF16),
                pltpu.VMEM((2, 2, HALO, ny, nz), F32),
                pltpu.VMEM((2, 5, nx, ny, nz), BF16),
                pltpu.VMEM((2, nx, ny, nz), F32),
                pltpu.VMEM((2, 2, 4, HALO, ny, nz), BF16),
                pltpu.VMEM((2, 2, HALO, ny, nz), F32),
                pltpu.VMEM((2, 5, ny, nz), BF16),
                pltpu.VMEM((2, ny, nz), F32),
                pltpu.VMEM((2, 3, 2, 5, ny, nz), BF16),
                pltpu.VMEM((2, 3, 2, ny, nz), F32),
                pltpu.VMEM((5, nx, ny, nz), BF16),
                pltpu.VMEM((nx, ny, nz), F32),
                pltpu.VMEM((5, px) + wide, F32),
                pltpu.VMEM((3, px) + wide, F32),
                pltpu.VMEM((px,) + wide, F32),
                pltpu.VMEM((7, px) + wide, F32),
                pltpu.VMEM((px,) + wide, F32),
                pltpu.VMEM((px,) + wide, F32),
                pltpu.VMEM((5, nx, ny, nz), F32),
                pltpu.SemaphoreType.DMA((2, 24)),
                pltpu.SemaphoreType.DMA((2, 24)),
            ],
            compiler_params=pltpu.CompilerParams(collective_id=0, has_side_effects=True),
        )(conserved, sigma_prev)

    return jax.shard_map(
        step,
        mesh=mesh,
        in_specs=(P(None, "gx", "gy", "gz"), P("gx", "gy", "gz")),
        out_specs=(P(None, "gx", "gy", "gz"), P("gx", "gy", "gz")),
        check_vma=False,
    )
```

```python
import functools

import jax
import jax.numpy as jnp
from jax import lax
from jax.experimental import pallas as pl
from jax.experimental.pallas import tpu as pltpu
from jax.sharding import PartitionSpec as P

SWEEPS = 4
HALO = SWEEPS + 1
REACH = 3
gamma_gas = 1.4
alpha_reg = 4.0
time_step = 0.08
MESH = pl.DeviceIdType.MESH
F32 = jnp.float32
BF16 = jnp.bfloat16


def edges(c, p1, m1, p2, m2):
    even = (47.0 / 60.0) * c + (7.0 / 60.0) * (p1 + m1) - (0.5 / 60.0) * (p2 + m2)
    odd = (20.0 / 60.0) * (p1 - m1) - (2.5 / 60.0) * (p2 - m2)
    return even + odd, even - odd


def physical_flux(v, d):
    inv = 1.0 / v[0]
    u = [v[1] * inv, v[2] * inv, v[3] * inv]
    kinetic = 0.5 * (v[1] * u[0] + v[2] * u[1] + v[3] * u[2])
    p = (gamma_gas - 1.0) * (v[4] - kinetic)
    n = u[d]
    flux = [v[1 + d], v[1] * n, v[2] * n, v[3] * n, (v[4] + p) * n]
    flux[1 + d] = flux[1 + d] + p
    return flux, jnp.abs(n) + jnp.sqrt(gamma_gas * jnp.abs(p) * inv)


def face_flux(left, right, d):
    fl, sl = physical_flux(left, d)
    fr, sr = physical_flux(right, d)
    speed = jnp.maximum(sl, sr)
    return [0.5 * ((a + b) - speed * (r - l)) for a, b, l, r in zip(fl, fr, left, right)]


def up(v, axis, by=1):
    return pltpu.roll(v, (v.shape[axis] - by) % v.shape[axis], axis)


def down(v, axis, by=1):
    return pltpu.roll(v, by, axis)


def kernel(counts, cons, sigma, new_out, ent_out, xq, xe, xs, yq, ys, yxq, yxs, pq, ps, rq, rs,
           stq, sts, QF, U, INV, CO, SA, SB, WQ, WU, WI, WC, WA, WB, ZB, T, send_sem, recv_sem):
    gx, gy, gz = lax.axis_index("gx"), lax.axis_index("gy"), lax.axis_index("gz")
    nx, ny, nz = sigma.shape
    px = nx + 2 * HALO
    slot = nz // nx
    half = slot // 2
    own_y, far_y = slice(0, ny), slice(ny, 2 * ny)

    def dev(dx, dy, dz):
        return (
            lax.rem(gx + dx + counts[0], counts[0]),
            lax.rem(gy + dy, counts[1]),
            lax.rem(gz + dz, counts[2]),
        )

    lane = lax.broadcasted_iota(jnp.int32, (ny, nz), 1)
    lane2 = lax.broadcasted_iota(jnp.int32, (2 * ny, nz), 1)
    lower = (lane & (slot - 1)) < half
    lower2 = (lane2 & (slot - 1)) < half

    def pack(sec, q, s):
        for f in range(6):
            acc = None
            for k in range(nx):
                v = q[f, k].astype(F32) if f < 5 else s[k]
                r = pltpu.roll(v, (half + slot * k) % nz, 1)
                acc = r if acc is None else jnp.where(lane >= slot * k, r, acc)
            if f < 5:
                pq[sec, f] = acc.astype(BF16)
            else:
                ps[sec] = acc

    peers = [(-1, 0, 0), (1, 0, 0), (0, 1, 0), (0, 0, 1), (0, 1, 1), (-1, 0, 1), (1, 0, 1)]

    def x_next(v, g, after):
        r = up(v, 1, slot)
        return r if after is None else jnp.where(lane2 >= nz - slot, up(after, 1, slot), r)

    def x_prev(v, g, before):
        r = down(v, 1, slot)
        return r if before is None else jnp.where(lane2 < slot, down(before, 1, slot), r)

    def section(sec, carry):
        q, s = stq.at[sec], sts.at[sec]
        number = [0]
        everything = []

        def copy(src, dst, where):
            k = number[0]
            number[0] += 1
            c = pltpu.make_async_remote_copy(
                src_ref=src, dst_ref=dst, send_sem=send_sem.at[sec, k],
                recv_sem=recv_sem.at[sec, k], device_id=dev(*where), device_id_type=MESH,
            )
            everything.append(c)
            return c

        x_copies = []
        for side in (0, 1):
            to = (1, 0, 0) if side == 0 else (-1, 0, 0)
            a = nx - HALO if side == 0 else 0
            b = nx - REACH if side == 0 else 0
            x_copies.append([
                copy(q.at[0:4, a:a + HALO], xq.at[sec, side], to),
                copy(s.at[a:a + HALO], xs.at[sec, side], to),
                copy(q.at[4, b:b + REACH], xe.at[sec, side], to),
            ])
        y_copies = [copy(q, yq.at[sec], (0, 1, 0)), copy(s, ys.at[sec], (0, 1, 0))]
        relays = [
            [copy(xq.at[sec, side], yxq.at[sec, side], (0, 1, 0)),
             copy(xs.at[sec, side], yxs.at[sec, side], (0, 1, 0))]
            for side in (0, 1)
        ]
        packs, pack_relays = {}, {}
        for dx, dy, dz in ((0, 0, 1), (0, 1, 0), (0, 1, 1)):
            packs[(dy, dz, 1)] = [
                copy(pq.at[sec], rq.at[sec, dy, dz, 1], (dx, dy, dz)),
                copy(ps.at[sec], rs.at[sec, dy, dz, 1], (dx, dy, dz)),
            ]
        for dz in (0, 1):
            for dx in (1, -1):
                j = 1 - dx
                packs[(0, dz, j)] = [
                    copy(pq.at[sec, 0:4], rq.at[sec, 0, dz, j, 0:4], (dx, 0, dz)),
                    copy(ps.at[sec], rs.at[sec, 0, dz, j], (dx, 0, dz)),
                ]
                pack_relays[(dz, j)] = [
                    copy(rq.at[sec, 0, dz, j, 0:4], rq.at[sec, 1, dz, j, 0:4], (0, 1, 0)),
                    copy(rs.at[sec, 0, dz, j], rs.at[sec, 1, dz, j], (0, 1, 0)),
                ]

        for pair in x_copies:
            for c in pair:
                c.start()
        for c in y_copies:
            c.start()
        pack(sec, q, s)
        for both in packs.values():
            for c in both:
                c.start()

        for k in range(nx):
            for f in range(5):
                QF[f, HALO + k, own_y] = q[f, k].astype(F32)
            SA[HALO + k, own_y] = s[k]

        def windows(g, dy, fields):
            rows = far_y if dy else own_y
            for f in range(fields + 1):
                if f < fields:
                    own = pq[sec, f] if (g, dy) == (1, 0) else rq[sec, dy, 0, g, f]
                    own, far = own.astype(F32), rq[sec, dy, 1, g, f].astype(F32)
                    WQ[f, 2 * g, rows] = jnp.where(lower, far, own)
                    WQ[f, 2 * g + 1, rows] = jnp.where(lower, own, far)
                else:
                    own = ps[sec] if (g, dy) == (1, 0) else rs[sec, dy, 0, g]
                    far = rs[sec, dy, 1, g]
                    WA[2 * g, rows] = jnp.where(lower, far, own)
                    WA[2 * g + 1, rows] = jnp.where(lower, own, far)

        for c in y_copies:
            c.wait_recv()
        for k in range(nx):
            for f in range(5):
                QF[f, HALO + k, far_y] = yq[sec, f, k].astype(F32)
            SA[HALO + k, far_y] = ys[sec, k]
        for which in ((0, 1, 1), (1, 0, 1), (1, 1, 1)):
            for c in packs[which]:
                c.wait_recv()
        windows(1, 0, 5)
        windows(1, 1, 4)

        def line_flux(fields, d, axis):
            left, right = [], []
            for c in fields:
                l, r = edges(c, up(c, axis), down(c, axis), up(c, axis, 2), down(c, axis, 2))
                left.append(l)
                right.append(up(r, axis))
            return [v - down(v, axis) for v in face_flux(left, right, d)]

        lo = line_flux([WQ[f, 2, own_y] for f in range(5)], 2, 1)
        hi = line_flux([WQ[f, 3, own_y] for f in range(5)], 2, 1)
        for f in range(5):
            ZB[f] = jnp.where(lower, hi[f], lo[f])

        near = jnp.logical_or(lane < REACH, lane >= nz - REACH)

        def side_flux(k, carry):
            p = HALO + k
            ychange = line_flux([QF[f, p] for f in range(5)], 1, 0)
            zchange = line_flux([QF[f, p, own_y] for f in range(5)], 2, 1)
            shift = nz - half - slot * k
            for f in range(5):
                z = jnp.where(near, pltpu.roll(ZB[f], shift, 1), zchange[f])
                T[f, k] = ychange[f][own_y] + z
            return carry

        lax.fori_loop(0, nx, side_flux, 0)

        for side in (0, 1):
            for c in x_copies[side]:
                c.wait_recv()
            for c in relays[side]:
                c.start()
        for (dz, j), both in pack_relays.items():
            for c in packs[(0, dz, j)]:
                c.wait_recv()
            for c in both:
                c.start()
        for side in (0, 1):
            base = 0 if side == 0 else HALO + nx
            ebase = HALO - REACH if side == 0 else HALO + nx
            for k in range(HALO):
                for f in range(4):
                    QF[f, base + k, own_y] = xq[sec, side, f, k].astype(F32)
                SA[base + k, own_y] = xs[sec, side, k]
            for k in range(REACH):
                QF[4, ebase + k, own_y] = xe[sec, side, k].astype(F32)

        def x_face(p):
            left, right = [], []
            for f in range(5):
                v = [QF[f, p + o, own_y] for o in range(-2, 4)]
                left.append(edges(v[2], v[3], v[1], v[4], v[0])[0])
                right.append(edges(v[3], v[4], v[2], v[5], v[1])[1])
            return face_flux(left, right, 0)

        def x_flux(k, before):
            h = x_face(HALO + k)
            for f in range(5):
                T[f, k] = T[f, k] + (h[f] - before[f])
            return tuple(h)

        lax.fori_loop(0, nx, x_flux, tuple(x_face(HALO - 1)), unroll=2)

        windows(0, 0, 4)
        windows(2, 0, 4)
        for side in (0, 1):
            base = 0 if side == 0 else HALO + nx
            for c in relays[side]:
                c.wait_recv()
            for k in range(HALO):
                for f in range(4):
                    QF[f, base + k, far_y] = yxq[sec, side, f, k].astype(F32)
                SA[base + k, far_y] = yxs[sec, side, k]
        for both in pack_relays.values():
            for c in both:
                c.wait_recv()
        windows(0, 1, 4)
        windows(2, 1, 4)

        def velocities(p, carry):
            inv = 1.0 / QF[0, p]
            INV[p] = inv
            for a in range(3):
                U[a, p] = QF[1 + a, p] * inv
            return carry

        lax.fori_loop(0, px, velocities, 0, unroll=3)
        for n in range(6):
            inv = 1.0 / WQ[0, n]
            WI[n] = inv
            for a in range(3):
                WU[a, n] = WQ[1 + a, n] * inv

        def stencil_terms(g, c, around):
            div = g[0][0] + g[1][1] + g[2][2]
            total = div * div + g[0][0] * g[0][0] + g[1][1] * g[1][1] + g[2][2] * g[2][2]
            total = total + 2.0 * (g[0][1] * g[1][0] + g[0][2] * g[2][0] + g[1][2] * g[2][1])
            source = (alpha_reg * 0.25) * total
            w = [(alpha_reg * 0.5) * (c + n) for n in around]
            scale = 1.0 / (c + ((w[0] + w[1]) + (w[2] + w[3]) + (w[4] + w[5])))
            return [v * scale for v in w] + [source * scale]

        def coefficients(p, carry):
            g = []
            for a in range(3):
                u = U[a, p]
                g.append([
                    U[a, p + 1] - U[a, p - 1], up(u, 0) - down(u, 0), up(u, 1) - down(u, 1),
                ])
            c = INV[p]
            around = [INV[p + 1], INV[p - 1], up(c, 0), down(c, 0), up(c, 1), down(c, 1)]
            for n, v in enumerate(stencil_terms(g, c, around)):
                CO[n, p] = v
            return carry

        lax.fori_loop(1, px - 1, coefficients, 0, unroll=2)

        def in_x(ref, n):
            v = ref[n]
            after = ref[n + 2] if n < 4 else None
            before = ref[n - 2] if n > 1 else None
            return x_next(v, n, after), x_prev(v, n, before)

        for n in range(6):
            g = []
            for a in range(3):
                u = WU[a, n]
                hi_x, lo_x = in_x(WU.at[a], n)
                g.append([hi_x - lo_x, up(u, 0) - down(u, 0), up(u, 1) - down(u, 1)])
            c = WI[n]
            around = list(in_x(WI, n)) + [up(c, 0), down(c, 0), up(c, 1), down(c, 1)]
            for m, v in enumerate(stencil_terms(g, c, around)):
                WC[m, n] = v

        def jacobi(co, c, xp, xm):
            out = co(6) + co(0) * xp + co(1) * xm
            out = out + (co(2) * up(c, 0) + co(3) * down(c, 0))
            return out + (co(4) * up(c, 1) + co(5) * down(c, 1))

        read, write = SA, SB
        wread, wwrite = WA, WB
        for step in range(SWEEPS):
            def one(p, carry, read=read, write=write):
                write[p] = jacobi(lambda m: CO[m, p], read[p], read[p + 1], read[p - 1])
                return carry

            lax.fori_loop(step + 1, px - 1 - step, one, 0, unroll=2)
            for n in range(6):
                xp, xm = in_x(wread, n)
                wwrite[n] = jacobi(lambda m: WC[m, n], wread[n], xp, xm)
            read, write = write, read
            wread, wwrite = wwrite, wread
        S, WS = read, wread

        edge = jnp.logical_or(lane2 < SWEEPS, lane2 >= nz - SWEEPS)
        joined = [jnp.where(lower2, WS[2 * g + 1], WS[2 * g]) for g in range(3)]
        for k in range(-1, nx + 1):
            p = HALO + k
            g, at = (k + nx) // nx, (k + nx) % nx
            S[p] = jnp.where(edge, pltpu.roll(joined[g], nz - half - slot * at, 1), S[p])
        diffs = []
        for n in (2, 3):
            v = WS[n, own_y]
            e = v * WU[2, n, own_y]
            diffs.append((up(v, 1) - down(v, 1), up(e, 1) - down(e, 1)))
        for i in (0, 1):
            ZB[i] = jnp.where(lower, diffs[1][i], diffs[0][i])
        ends = jnp.logical_or(lane == 0, lane == nz - 1)

        def finish(k, carry):
            p = HALO + k
            shift = nz - half - slot * k
            push = [T[f, k] for f in range(5)]
            xp, xm = S[p + 1, own_y], S[p - 1, own_y]
            push[1] = push[1] + 0.5 * (xp - xm)
            power = xp * U[0, p + 1, own_y] - xm * U[0, p - 1, own_y]
            sy = S[p]
            push[2] = push[2] + 0.5 * (up(sy, 0) - down(sy, 0))[own_y]
            e = sy * U[1, p]
            power = power + (up(e, 0) - down(e, 0))[own_y]
            sz = S[p, own_y]
            dz = jnp.where(ends, pltpu.roll(ZB[0], shift, 1), up(sz, 1) - down(sz, 1))
            push[3] = push[3] + 0.5 * dz
            e = sz * U[2, p, own_y]
            power = power + jnp.where(ends, pltpu.roll(ZB[1], shift, 1), up(e, 1) - down(e, 1))
            push[4] = push[4] + 0.5 * power
            for f in range(5):
                initial = cons[f, k].astype(F32)
                moved = initial - time_step * push[f]
                new_out[f, k] = 0.5 * (moved + q[f, k].astype(F32))
                stq[sec + 1, f, k] = moved.astype(BF16)
            ent_out[k] = sz
            sts[sec + 1, k] = sz
            return carry

        lax.fori_loop(0, nx, finish, 0, unroll=2)
        for c in everything:
            c.wait_send()
        return carry

    stq[0] = cons[...]
    sts[0] = sigma[...]
    barrier = pltpu.get_barrier_semaphore()
    for peer in peers:
        pl.semaphore_signal(barrier, inc=1, device_id=dev(*peer), device_id_type=MESH)
    pl.semaphore_wait(barrier, len(peers))
    lax.fori_loop(0, 2, section, 0)


def slot_ok(nz, nx):
    return nz % nx == 0 and (nz // nx) & (nz // nx - 1) == 0


def solution(mesh):
    counts = (mesh.shape["gx"], mesh.shape["gy"], mesh.shape["gz"])
    assert counts[1] == 2 and counts[2] == 2

    def step(conserved, sigma_prev):
        _, nx, ny, nz = conserved.shape
        px = nx + 2 * HALO
        wide = (2 * ny, nz)
        assert nx >= HALO and nz // nx >= 4 * SWEEPS and slot_ok(nz, nx)
        vmem = pl.BlockSpec(memory_space=pltpu.VMEM)
        return pl.pallas_call(
            functools.partial(kernel, counts),
            out_shape=(
                jax.ShapeDtypeStruct((5, nx, ny, nz), F32),
                jax.ShapeDtypeStruct((nx, ny, nz), F32),
            ),
            in_specs=[vmem, vmem],
            out_specs=(vmem, vmem),
            scratch_shapes=[
                pltpu.VMEM((2, 2, 4, HALO, ny, nz), BF16),
                pltpu.VMEM((2, 2, REACH, ny, nz), BF16),
                pltpu.VMEM((2, 2, HALO, ny, nz), F32),
                pltpu.VMEM((2, 5, nx, ny, nz), BF16),
                pltpu.VMEM((2, nx, ny, nz), F32),
                pltpu.VMEM((2, 2, 4, HALO, ny, nz), BF16),
                pltpu.VMEM((2, 2, HALO, ny, nz), F32),
                pltpu.VMEM((2, 5, ny, nz), BF16),
                pltpu.VMEM((2, ny, nz), F32),
                pltpu.VMEM((2, 2, 2, 3, 5, ny, nz), BF16),
                pltpu.VMEM((2, 2, 2, 3, ny, nz), F32),
                pltpu.VMEM((3, 5, nx, ny, nz), BF16),
                pltpu.VMEM((3, nx, ny, nz), F32),
                pltpu.VMEM((5, px) + wide, F32),
                pltpu.VMEM((3, px) + wide, F32),
                pltpu.VMEM((px,) + wide, F32),
                pltpu.VMEM((7, px) + wide, F32),
                pltpu.VMEM((px,) + wide, F32),
                pltpu.VMEM((px,) + wide, F32),
                pltpu.VMEM((5, 6) + wide, F32),
                pltpu.VMEM((3, 6) + wide, F32),
                pltpu.VMEM((6,) + wide, F32),
                pltpu.VMEM((7, 6) + wide, F32),
                pltpu.VMEM((6,) + wide, F32),
                pltpu.VMEM((6,) + wide, F32),
                pltpu.VMEM((5, ny, nz), F32),
                pltpu.VMEM((5, nx, ny, nz), F32),
                pltpu.SemaphoreType.DMA((2, 34)),
                pltpu.SemaphoreType.DMA((2, 34)),
            ],
            compiler_params=pltpu.CompilerParams(collective_id=0, has_side_effects=True),
        )(conserved, sigma_prev)

    return jax.shard_map(
        step,
        mesh=mesh,
        in_specs=(P(None, "gx", "gy", "gz"), P("gx", "gy", "gz")),
        out_specs=(P(None, "gx", "gy", "gz"), P("gx", "gy", "gz")),
        check_vma=False,
    )
```

```python
import functools

import jax
import jax.numpy as jnp
from jax import lax
from jax.experimental import pallas as pl
from jax.experimental.pallas import tpu as pltpu
from jax.sharding import PartitionSpec as P

SWEEPS = 4
HALO = SWEEPS + 1
REACH = 3
gamma_gas = 1.4
alpha_reg = 4.0
time_step = 0.08
MESH = pl.DeviceIdType.MESH
F32 = jnp.float32
BF16 = jnp.bfloat16


def edges(c, p1, m1, p2, m2):
    even = (47.0 / 60.0) * c + (7.0 / 60.0) * (p1 + m1) - (0.5 / 60.0) * (p2 + m2)
    odd = (20.0 / 60.0) * (p1 - m1) - (2.5 / 60.0) * (p2 - m2)
    return even + odd, even - odd


def physical_flux(v, d):
    inv = 1.0 / v[0]
    u = [v[1] * inv, v[2] * inv, v[3] * inv]
    kinetic = 0.5 * (v[1] * u[0] + v[2] * u[1] + v[3] * u[2])
    p = (gamma_gas - 1.0) * (v[4] - kinetic)
    n = u[d]
    flux = [v[1 + d], v[1] * n, v[2] * n, v[3] * n, (v[4] + p) * n]
    flux[1 + d] = flux[1 + d] + p
    return flux, jnp.abs(n) + jnp.sqrt(gamma_gas * jnp.abs(p) * inv)


def face_flux(left, right, d):
    fl, sl = physical_flux(left, d)
    fr, sr = physical_flux(right, d)
    speed = jnp.maximum(sl, sr)
    return [0.5 * ((a + b) - speed * (r - l)) for a, b, l, r in zip(fl, fr, left, right)]


def up(v, axis, by=1):
    return pltpu.roll(v, (v.shape[axis] - by) % v.shape[axis], axis)


def down(v, axis, by=1):
    return pltpu.roll(v, by, axis)


def kernel(counts, cons, sigma, new_out, ent_out, xq, xe, xs, yq, ys, yxq, yxs, pq, ps, rq, rs,
           stq, sts, QF, U, INV, CO, SA, SB, WQ, WU, WI, WC, WA, WB, ZB, T, send_sem, recv_sem):
    gx, gy, gz = lax.axis_index("gx"), lax.axis_index("gy"), lax.axis_index("gz")
    nx, ny, nz = sigma.shape
    px = nx + 2 * HALO
    slot = nz // nx
    half = slot // 2
    own_y, far_y = slice(0, ny), slice(ny, 2 * ny)

    def dev(dx, dy, dz):
        return (
            lax.rem(gx + dx + counts[0], counts[0]),
            lax.rem(gy + dy, counts[1]),
            lax.rem(gz + dz, counts[2]),
        )

    lane = lax.broadcasted_iota(jnp.int32, (ny, nz), 1)
    lane2 = lax.broadcasted_iota(jnp.int32, (2 * ny, nz), 1)
    lower = (lane & (slot - 1)) < half
    lower2 = (lane2 & (slot - 1)) < half

    def pack(sec, q, s):
        for f in range(6):
            acc = None
            for k in range(nx):
                v = q[f, k].astype(F32) if f < 5 else s[k]
                r = pltpu.roll(v, (half + slot * k) % nz, 1)
                acc = r if acc is None else jnp.where(lane >= slot * k, r, acc)
            if f < 5:
                pq[sec, f] = acc.astype(BF16)
            else:
                ps[sec] = acc

    peers = [(-1, 0, 0), (1, 0, 0), (0, 1, 0), (0, 0, 1), (0, 1, 1), (-1, 0, 1), (1, 0, 1)]

    def x_next(v, g, after):
        r = up(v, 1, slot)
        return r if after is None else jnp.where(lane2 >= nz - slot, up(after, 1, slot), r)

    def x_prev(v, g, before):
        r = down(v, 1, slot)
        return r if before is None else jnp.where(lane2 < slot, down(before, 1, slot), r)

    def section(sec, carry):
        q, s = stq.at[sec], sts.at[sec]
        number = [0]
        everything = []

        def copy(src, dst, where):
            k = number[0]
            number[0] += 1
            c = pltpu.make_async_remote_copy(
                src_ref=src, dst_ref=dst, send_sem=send_sem.at[sec, k],
                recv_sem=recv_sem.at[sec, k], device_id=dev(*where), device_id_type=MESH,
            )
            everything.append(c)
            return c

        x_copies = []
        for side in (0, 1):
            to = (1, 0, 0) if side == 0 else (-1, 0, 0)
            a = nx - HALO if side == 0 else 0
            b = nx - REACH if side == 0 else 0
            x_copies.append([
                copy(q.at[0:4, a:a + HALO], xq.at[sec, side], to),
                copy(s.at[a:a + HALO], xs.at[sec, side], to),
                copy(q.at[4, b:b + REACH], xe.at[sec, side], to),
            ])
        y_copies = [copy(q, yq.at[sec], (0, 1, 0)), copy(s, ys.at[sec], (0, 1, 0))]
        relays = [
            [copy(xq.at[sec, side], yxq.at[sec, side], (0, 1, 0)),
             copy(xs.at[sec, side], yxs.at[sec, side], (0, 1, 0))]
            for side in (0, 1)
        ]
        packs, pack_relays = {}, {}
        for dx, dy, dz in ((0, 0, 1), (0, 1, 0), (0, 1, 1)):
            packs[(dy, dz, 1)] = [
                copy(pq.at[sec], rq.at[sec, dy, dz, 1], (dx, dy, dz)),
                copy(ps.at[sec], rs.at[sec, dy, dz, 1], (dx, dy, dz)),
            ]
        for dz in (0, 1):
            for dx in (1, -1):
                j = 1 - dx
                packs[(0, dz, j)] = [
                    copy(pq.at[sec, 0:4], rq.at[sec, 0, dz, j, 0:4], (dx, 0, dz)),
                    copy(ps.at[sec], rs.at[sec, 0, dz, j], (dx, 0, dz)),
                ]
                pack_relays[(dz, j)] = [
                    copy(rq.at[sec, 0, dz, j, 0:4], rq.at[sec, 1, dz, j, 0:4], (0, 1, 0)),
                    copy(rs.at[sec, 0, dz, j], rs.at[sec, 1, dz, j], (0, 1, 0)),
                ]

        for pair in x_copies:
            for c in pair:
                c.start()
        for c in y_copies:
            c.start()
        pack(sec, q, s)
        for both in packs.values():
            for c in both:
                c.start()

        for k in range(nx):
            for f in range(5):
                QF[f, HALO + k, own_y] = q[f, k].astype(F32)
            SA[HALO + k, own_y] = s[k]

        def windows(g, dy, fields):
            rows = far_y if dy else own_y
            for f in range(fields + 1):
                if f < fields:
                    own = pq[sec, f] if (g, dy) == (1, 0) else rq[sec, dy, 0, g, f]
                    own, far = own.astype(F32), rq[sec, dy, 1, g, f].astype(F32)
                    WQ[f, 2 * g, rows] = jnp.where(lower, far, own)
                    WQ[f, 2 * g + 1, rows] = jnp.where(lower, own, far)
                else:
                    own = ps[sec] if (g, dy) == (1, 0) else rs[sec, dy, 0, g]
                    far = rs[sec, dy, 1, g]
                    WA[2 * g, rows] = jnp.where(lower, far, own)
                    WA[2 * g + 1, rows] = jnp.where(lower, own, far)

        for c in y_copies:
            c.wait_recv()
        for k in range(nx):
            for f in range(5):
                QF[f, HALO + k, far_y] = yq[sec, f, k].astype(F32)
            SA[HALO + k, far_y] = ys[sec, k]
        for which in ((0, 1, 1), (1, 0, 1), (1, 1, 1)):
            for c in packs[which]:
                c.wait_recv()
        windows(1, 0, 5)
        windows(1, 1, 4)

        def line_flux(fields, d, axis):
            left, right = [], []
            for c in fields:
                l, r = edges(c, up(c, axis), down(c, axis), up(c, axis, 2), down(c, axis, 2))
                left.append(l)
                right.append(up(r, axis))
            return [v - down(v, axis) for v in face_flux(left, right, d)]

        lo = line_flux([WQ[f, 2, own_y] for f in range(5)], 2, 1)
        hi = line_flux([WQ[f, 3, own_y] for f in range(5)], 2, 1)
        for f in range(5):
            ZB[f] = jnp.where(lower, hi[f], lo[f])

        near = jnp.logical_or(lane < REACH, lane >= nz - REACH)

        def side_flux(k, carry):
            p = HALO + k
            ychange = line_flux([QF[f, p] for f in range(5)], 1, 0)
            zchange = line_flux([QF[f, p, own_y] for f in range(5)], 2, 1)
            shift = nz - half - slot * k
            for f in range(5):
                z = jnp.where(near, pltpu.roll(ZB[f], shift, 1), zchange[f])
                T[f, k] = ychange[f][own_y] + z
            return carry

        lax.fori_loop(0, nx, side_flux, 0, unroll=2)

        def velocities(p, carry):
            inv = 1.0 / QF[0, p]
            INV[p] = inv
            for a in range(3):
                U[a, p] = QF[1 + a, p] * inv
            return carry

        def stencil_terms(g, c, around):
            div = g[0][0] + g[1][1] + g[2][2]
            total = div * div + g[0][0] * g[0][0] + g[1][1] * g[1][1] + g[2][2] * g[2][2]
            total = total + 2.0 * (g[0][1] * g[1][0] + g[0][2] * g[2][0] + g[1][2] * g[2][1])
            source = (alpha_reg * 0.25) * total
            w = [(alpha_reg * 0.5) * (c + n) for n in around]
            scale = 1.0 / (c + ((w[0] + w[1]) + (w[2] + w[3]) + (w[4] + w[5])))
            return [v * scale for v in w] + [source * scale]

        def coefficients(p, carry):
            g = []
            for a in range(3):
                u = U[a, p]
                g.append([
                    U[a, p + 1] - U[a, p - 1], up(u, 0) - down(u, 0), up(u, 1) - down(u, 1),
                ])
            c = INV[p]
            around = [INV[p + 1], INV[p - 1], up(c, 0), down(c, 0), up(c, 1), down(c, 1)]
            for n, v in enumerate(stencil_terms(g, c, around)):
                CO[n, p] = v
            return carry

        def jacobi(co, c, xp, xm):
            out = co(6) + co(0) * xp + co(1) * xm
            out = out + (co(2) * up(c, 0) + co(3) * down(c, 0))
            return out + (co(4) * up(c, 1) + co(5) * down(c, 1))

        def main_sweep(step, planes):
            read, write = (SA, SB) if step % 2 == 0 else (SB, SA)
            for p in planes:
                write[p] = jacobi(lambda m: CO[m, p], read[p], read[p + 1], read[p - 1])

        inner = [range(HALO + 1 + t, HALO + nx - 1 - t) for t in range(SWEEPS)]
        lax.fori_loop(HALO, HALO + nx, velocities, 0, unroll=4)
        lax.fori_loop(inner[0].start, inner[0].stop, coefficients, 0, unroll=3)
        for step in range(SWEEPS):
            main_sweep(step, inner[step])

        for side in (0, 1):
            for c in x_copies[side]:
                c.wait_recv()
            for c in relays[side]:
                c.start()
        for (dz, j), both in pack_relays.items():
            for c in packs[(0, dz, j)]:
                c.wait_recv()
            for c in both:
                c.start()
        for side in (0, 1):
            base = 0 if side == 0 else HALO + nx
            ebase = HALO - REACH if side == 0 else HALO + nx
            for k in range(HALO):
                for f in range(4):
                    QF[f, base + k, own_y] = xq[sec, side, f, k].astype(F32)
                SA[base + k, own_y] = xs[sec, side, k]
            for k in range(REACH):
                QF[4, ebase + k, own_y] = xe[sec, side, k].astype(F32)

        def x_face(p):
            left, right = [], []
            for f in range(5):
                v = [QF[f, p + o, own_y] for o in range(-2, 4)]
                left.append(edges(v[2], v[3], v[1], v[4], v[0])[0])
                right.append(edges(v[3], v[4], v[2], v[5], v[1])[1])
            return face_flux(left, right, 0)

        def x_flux(k, before):
            h = x_face(HALO + k)
            for f in range(5):
                T[f, k] = T[f, k] + (h[f] - before[f])
            return tuple(h)

        lax.fori_loop(0, nx, x_flux, tuple(x_face(HALO - 1)), unroll=4)

        windows(0, 0, 4)
        windows(2, 0, 4)
        for side in (0, 1):
            base = 0 if side == 0 else HALO + nx
            for c in relays[side]:
                c.wait_recv()
            for k in range(HALO):
                for f in range(4):
                    QF[f, base + k, far_y] = yxq[sec, side, f, k].astype(F32)
                SA[base + k, far_y] = yxs[sec, side, k]
        for both in pack_relays.values():
            for c in both:
                c.wait_recv()
        windows(0, 1, 4)
        windows(2, 1, 4)

        for base in (0, HALO + nx):
            for p in range(base, base + HALO):
                velocities(p, 0)
        for n in range(6):
            inv = 1.0 / WQ[0, n]
            WI[n] = inv
            for a in range(3):
                WU[a, n] = WQ[1 + a, n] * inv

        for p in range(1, px - 1):
            if p not in inner[0]:
                coefficients(p, 0)

        def in_x(ref, n):
            v = ref[n]
            after = ref[n + 2] if n < 4 else None
            before = ref[n - 2] if n > 1 else None
            return x_next(v, n, after), x_prev(v, n, before)

        for n in range(6):
            g = []
            for a in range(3):
                u = WU[a, n]
                hi_x, lo_x = in_x(WU.at[a], n)
                g.append([hi_x - lo_x, up(u, 0) - down(u, 0), up(u, 1) - down(u, 1)])
            c = WI[n]
            around = list(in_x(WI, n)) + [up(c, 0), down(c, 0), up(c, 1), down(c, 1)]
            for m, v in enumerate(stencil_terms(g, c, around)):
                WC[m, n] = v

        wread, wwrite = WA, WB
        for step in range(SWEEPS):
            main_sweep(step, [p for p in range(step + 1, px - 1 - step) if p not in inner[step]])
            for n in range(6):
                xp, xm = in_x(wread, n)
                wwrite[n] = jacobi(lambda m: WC[m, n], wread[n], xp, xm)
            wread, wwrite = wwrite, wread
        S, WS = (SA if SWEEPS % 2 == 0 else SB), wread

        edge = jnp.logical_or(lane2 < SWEEPS, lane2 >= nz - SWEEPS)
        joined = [jnp.where(lower2, WS[2 * g + 1], WS[2 * g]) for g in range(3)]
        for k in range(-1, nx + 1):
            p = HALO + k
            g, at = (k + nx) // nx, (k + nx) % nx
            S[p] = jnp.where(edge, pltpu.roll(joined[g], nz - half - slot * at, 1), S[p])
        diffs = []
        for n in (2, 3):
            v = WS[n, own_y]
            e = v * WU[2, n, own_y]
            diffs.append((up(v, 1) - down(v, 1), up(e, 1) - down(e, 1)))
        for i in (0, 1):
            ZB[i] = jnp.where(lower, diffs[1][i], diffs[0][i])
        ends = jnp.logical_or(lane == 0, lane == nz - 1)

        def finish(k, carry):
            p = HALO + k
            shift = nz - half - slot * k
            push = [T[f, k] for f in range(5)]
            xp, xm = S[p + 1, own_y], S[p - 1, own_y]
            push[1] = push[1] + 0.5 * (xp - xm)
            power = xp * U[0, p + 1, own_y] - xm * U[0, p - 1, own_y]
            sy = S[p]
            push[2] = push[2] + 0.5 * (up(sy, 0) - down(sy, 0))[own_y]
            e = sy * U[1, p]
            power = power + (up(e, 0) - down(e, 0))[own_y]
            sz = S[p, own_y]
            dz = jnp.where(ends, pltpu.roll(ZB[0], shift, 1), up(sz, 1) - down(sz, 1))
            push[3] = push[3] + 0.5 * dz
            e = sz * U[2, p, own_y]
            power = power + jnp.where(ends, pltpu.roll(ZB[1], shift, 1), up(e, 1) - down(e, 1))
            push[4] = push[4] + 0.5 * power
            for f in range(5):
                initial = cons[f, k].astype(F32)
                moved = initial - time_step * push[f]
                new_out[f, k] = 0.5 * (moved + q[f, k].astype(F32))
                stq[sec + 1, f, k] = moved.astype(BF16)
            ent_out[k] = sz
            sts[sec + 1, k] = sz
            return carry

        lax.fori_loop(0, nx, finish, 0, unroll=4)
        for c in everything:
            c.wait_send()
        return carry

    stq[0] = cons[...]
    sts[0] = sigma[...]
    barrier = pltpu.get_barrier_semaphore()
    for peer in peers:
        pl.semaphore_signal(barrier, inc=1, device_id=dev(*peer), device_id_type=MESH)
    pl.semaphore_wait(barrier, len(peers))
    lax.fori_loop(0, 2, section, 0)


def slot_ok(nz, nx):
    return nz % nx == 0 and (nz // nx) & (nz // nx - 1) == 0


def solution(mesh):
    counts = (mesh.shape["gx"], mesh.shape["gy"], mesh.shape["gz"])
    assert counts[1] == 2 and counts[2] == 2

    def step(conserved, sigma_prev):
        _, nx, ny, nz = conserved.shape
        px = nx + 2 * HALO
        wide = (2 * ny, nz)
        assert nx >= HALO and nz // nx >= 4 * SWEEPS and slot_ok(nz, nx)
        vmem = pl.BlockSpec(memory_space=pltpu.VMEM)
        return pl.pallas_call(
            functools.partial(kernel, counts),
            out_shape=(
                pltpu.VMEM((5, nx, ny, nz), F32),
                pltpu.VMEM((nx, ny, nz), F32),
            ),
            in_specs=[vmem, vmem],
            out_specs=(vmem, vmem),
            scratch_shapes=[
                pltpu.VMEM((2, 2, 4, HALO, ny, nz), BF16),
                pltpu.VMEM((2, 2, REACH, ny, nz), BF16),
                pltpu.VMEM((2, 2, HALO, ny, nz), F32),
                pltpu.VMEM((2, 5, nx, ny, nz), BF16),
                pltpu.VMEM((2, nx, ny, nz), F32),
                pltpu.VMEM((2, 2, 4, HALO, ny, nz), BF16),
                pltpu.VMEM((2, 2, HALO, ny, nz), F32),
                pltpu.VMEM((2, 5, ny, nz), BF16),
                pltpu.VMEM((2, ny, nz), F32),
                pltpu.VMEM((2, 2, 2, 3, 5, ny, nz), BF16),
                pltpu.VMEM((2, 2, 2, 3, ny, nz), F32),
                pltpu.VMEM((3, 5, nx, ny, nz), BF16),
                pltpu.VMEM((3, nx, ny, nz), F32),
                pltpu.VMEM((5, px) + wide, F32),
                pltpu.VMEM((3, px) + wide, F32),
                pltpu.VMEM((px,) + wide, F32),
                pltpu.VMEM((7, px) + wide, F32),
                pltpu.VMEM((px,) + wide, F32),
                pltpu.VMEM((px,) + wide, F32),
                pltpu.VMEM((5, 6) + wide, F32),
                pltpu.VMEM((3, 6) + wide, F32),
                pltpu.VMEM((6,) + wide, F32),
                pltpu.VMEM((7, 6) + wide, F32),
                pltpu.VMEM((6,) + wide, F32),
                pltpu.VMEM((6,) + wide, F32),
                pltpu.VMEM((5, ny, nz), F32),
                pltpu.VMEM((5, nx, ny, nz), F32),
                pltpu.SemaphoreType.DMA((2, 34)),
                pltpu.SemaphoreType.DMA((2, 34)),
            ],
            compiler_params=pltpu.CompilerParams(collective_id=0, has_side_effects=True),
        )(conserved, sigma_prev)

    return jax.shard_map(
        step,
        mesh=mesh,
        in_specs=(P(None, "gx", "gy", "gz"), P("gx", "gy", "gz")),
        out_specs=(P(None, "gx", "gy", "gz"), P("gx", "gy", "gz")),
        check_vma=False,
    )
```

```python
import functools

import jax
import jax.numpy as jnp
from jax import lax
from jax.experimental import pallas as pl
from jax.experimental.pallas import tpu as pltpu
from jax.sharding import PartitionSpec as P

SWEEPS = 4
HALO = SWEEPS + 1
REACH = 3
gamma_gas = 1.4
alpha_reg = 4.0
time_step = 0.08
MESH = pl.DeviceIdType.MESH
F32 = jnp.float32
BF16 = jnp.bfloat16


def edges(c, p1, m1, p2, m2):
    even = (47.0 / 60.0) * c + (7.0 / 60.0) * (p1 + m1) - (0.5 / 60.0) * (p2 + m2)
    odd = (20.0 / 60.0) * (p1 - m1) - (2.5 / 60.0) * (p2 - m2)
    return even + odd, even - odd


def physical_flux(v, d):
    inv = 1.0 / v[0]
    u = [v[1] * inv, v[2] * inv, v[3] * inv]
    kinetic = 0.5 * (v[1] * u[0] + v[2] * u[1] + v[3] * u[2])
    p = (gamma_gas - 1.0) * (v[4] - kinetic)
    n = u[d]
    flux = [v[1 + d], v[1] * n, v[2] * n, v[3] * n, (v[4] + p) * n]
    flux[1 + d] = flux[1 + d] + p
    return flux, jnp.abs(n) + jnp.sqrt(gamma_gas * jnp.abs(p) * inv)


def face_flux(left, right, d):
    fl, sl = physical_flux(left, d)
    fr, sr = physical_flux(right, d)
    speed = jnp.maximum(sl, sr)
    return [0.5 * ((a + b) - speed * (r - l)) for a, b, l, r in zip(fl, fr, left, right)]


def up(v, axis, by=1):
    return pltpu.roll(v, (v.shape[axis] - by) % v.shape[axis], axis)


def down(v, axis, by=1):
    return pltpu.roll(v, by, axis)


def kernel(counts, cons, sigma, new_out, ent_out, xq, xe, xs, yq, ys, yxq, yxs, pq, ps, rq, rs,
           stq, sts, stb, QF, U, INV, CO, SA, SB, WQ, WU, WI, WC, WA, WB, ZB, T, send_sem, recv_sem):
    gx, gy, gz = lax.axis_index("gx"), lax.axis_index("gy"), lax.axis_index("gz")
    nx, ny, nz = sigma.shape
    px = nx + 2 * HALO
    slot = nz // nx
    half = slot // 2
    own_y, far_y = slice(0, ny), slice(ny, 2 * ny)

    def dev(dx, dy, dz):
        return (
            lax.rem(gx + dx + counts[0], counts[0]),
            lax.rem(gy + dy, counts[1]),
            lax.rem(gz + dz, counts[2]),
        )

    lane = lax.broadcasted_iota(jnp.int32, (ny, nz), 1)
    lane2 = lax.broadcasted_iota(jnp.int32, (2 * ny, nz), 1)
    lower = (lane & (slot - 1)) < half
    lower2 = (lane2 & (slot - 1)) < half

    def pack(sec, q, s):
        for f in range(6):
            acc = None
            for k in range(nx):
                v = q[f, k].astype(F32) if f < 5 else s[k]
                r = pltpu.roll(v, (half + slot * k) % nz, 1)
                acc = r if acc is None else jnp.where(lane >= slot * k, r, acc)
            if f < 5:
                pq[sec, f] = acc.astype(BF16)
            else:
                ps[sec] = acc

    peers = [(-1, 0, 0), (1, 0, 0), (0, 1, 0), (0, 0, 1), (0, 1, 1), (-1, 0, 1), (1, 0, 1)]

    def x_next(v, g, after):
        r = up(v, 1, slot)
        return r if after is None else jnp.where(lane2 >= nz - slot, up(after, 1, slot), r)

    def x_prev(v, g, before):
        r = down(v, 1, slot)
        return r if before is None else jnp.where(lane2 < slot, down(before, 1, slot), r)

    def section(sec, carry):
        q, s = stq.at[sec], sts.at[sec]
        number = [0]
        everything = []

        def copy(src, dst, where):
            k = number[0]
            number[0] += 1
            c = pltpu.make_async_remote_copy(
                src_ref=src, dst_ref=dst, send_sem=send_sem.at[sec, k],
                recv_sem=recv_sem.at[sec, k], device_id=dev(*where), device_id_type=MESH,
            )
            everything.append(c)
            return c

        x_copies = []
        for side in (0, 1):
            to = (1, 0, 0) if side == 0 else (-1, 0, 0)
            a = nx - HALO if side == 0 else 0
            b = nx - REACH if side == 0 else 0
            x_copies.append([
                copy(q.at[0:4, a:a + HALO], xq.at[sec, side], to),
                copy(stb.at[sec, a:a + HALO], xs.at[sec, side], to),
                copy(q.at[4, b:b + REACH], xe.at[sec, side], to),
            ])
        y_copies = [copy(q, yq.at[sec], (0, 1, 0)), copy(s, ys.at[sec], (0, 1, 0))]
        relays = [
            [copy(xq.at[sec, side], yxq.at[sec, side], (0, 1, 0)),
             copy(xs.at[sec, side], yxs.at[sec, side], (0, 1, 0))]
            for side in (0, 1)
        ]
        packs, pack_relays = {}, {}
        for dx, dy, dz in ((0, 0, 1), (0, 1, 0), (0, 1, 1)):
            packs[(dy, dz, 1)] = [
                copy(pq.at[sec], rq.at[sec, dy, dz, 1], (dx, dy, dz)),
                copy(ps.at[sec], rs.at[sec, dy, dz, 1], (dx, dy, dz)),
            ]
        for dz in (0, 1):
            for dx in (1, -1):
                j = 1 - dx
                packs[(0, dz, j)] = [
                    copy(pq.at[sec, 0:4], rq.at[sec, 0, dz, j, 0:4], (dx, 0, dz)),
                    copy(ps.at[sec], rs.at[sec, 0, dz, j], (dx, 0, dz)),
                ]
                pack_relays[(dz, j)] = [
                    copy(rq.at[sec, 0, dz, j, 0:4], rq.at[sec, 1, dz, j, 0:4], (0, 1, 0)),
                    copy(rs.at[sec, 0, dz, j], rs.at[sec, 1, dz, j], (0, 1, 0)),
                ]

        for pair in x_copies:
            for c in pair:
                c.start()
        for c in y_copies:
            c.start()
        pack(sec, q, s)
        for both in packs.values():
            for c in both:
                c.start()

        for k in range(nx):
            for f in range(5):
                QF[f, HALO + k, own_y] = q[f, k].astype(F32)
            SA[HALO + k, own_y] = s[k]

        def windows(g, dy, fields):
            rows = far_y if dy else own_y
            for f in range(fields + 1):
                if f < fields:
                    own = pq[sec, f] if (g, dy) == (1, 0) else rq[sec, dy, 0, g, f]
                    own, far = own.astype(F32), rq[sec, dy, 1, g, f].astype(F32)
                    WQ[f, 2 * g, rows] = jnp.where(lower, far, own)
                    WQ[f, 2 * g + 1, rows] = jnp.where(lower, own, far)
                else:
                    own = ps[sec] if (g, dy) == (1, 0) else rs[sec, dy, 0, g]
                    far = rs[sec, dy, 1, g]
                    WA[2 * g, rows] = jnp.where(lower, far, own)
                    WA[2 * g + 1, rows] = jnp.where(lower, own, far)

        for c in y_copies:
            c.wait_recv()
        for k in range(nx):
            for f in range(5):
                QF[f, HALO + k, far_y] = yq[sec, f, k].astype(F32)
            SA[HALO + k, far_y] = ys[sec, k]
        for which in ((0, 1, 1), (1, 0, 1), (1, 1, 1)):
            for c in packs[which]:
                c.wait_recv()
        windows(1, 0, 5)
        windows(1, 1, 4)

        def line_flux(fields, d, axis):
            left, right = [], []
            for c in fields:
                l, r = edges(c, up(c, axis), down(c, axis), up(c, axis, 2), down(c, axis, 2))
                left.append(l)
                right.append(up(r, axis))
            return [v - down(v, axis) for v in face_flux(left, right, d)]

        lo = line_flux([WQ[f, 2, own_y] for f in range(5)], 2, 1)
        hi = line_flux([WQ[f, 3, own_y] for f in range(5)], 2, 1)
        for f in range(5):
            ZB[f] = jnp.where(lower, hi[f], lo[f])

        near = jnp.logical_or(lane < REACH, lane >= nz - REACH)

        def side_flux(k, carry):
            p = HALO + k
            ychange = line_flux([QF[f, p] for f in range(5)], 1, 0)
            zchange = line_flux([QF[f, p, own_y] for f in range(5)], 2, 1)
            shift = nz - half - slot * k
            for f in range(5):
                z = jnp.where(near, pltpu.roll(ZB[f], shift, 1), zchange[f])
                T[f, k] = ychange[f][own_y] + z
            return carry

        lax.fori_loop(0, nx, side_flux, 0, unroll=2)

        def velocities(p, carry):
            inv = 1.0 / QF[0, p]
            INV[p] = inv
            for a in range(3):
                U[a, p] = QF[1 + a, p] * inv
            return carry

        def stencil_terms(g, c, around):
            div = g[0][0] + g[1][1] + g[2][2]
            total = div * div + g[0][0] * g[0][0] + g[1][1] * g[1][1] + g[2][2] * g[2][2]
            total = total + 2.0 * (g[0][1] * g[1][0] + g[0][2] * g[2][0] + g[1][2] * g[2][1])
            source = (alpha_reg * 0.25) * total
            w = [(alpha_reg * 0.5) * (c + n) for n in around]
            scale = 1.0 / (c + ((w[0] + w[1]) + (w[2] + w[3]) + (w[4] + w[5])))
            return [v * scale for v in w] + [source * scale]

        def coefficients(p, carry):
            g = []
            for a in range(3):
                u = U[a, p]
                g.append([
                    U[a, p + 1] - U[a, p - 1], up(u, 0) - down(u, 0), up(u, 1) - down(u, 1),
                ])
            c = INV[p]
            around = [INV[p + 1], INV[p - 1], up(c, 0), down(c, 0), up(c, 1), down(c, 1)]
            for n, v in enumerate(stencil_terms(g, c, around)):
                CO[n, p] = v
            return carry

        def jacobi(co, c, xp, xm):
            out = co(6) + co(0) * xp + co(1) * xm
            out = out + (co(2) * up(c, 0) + co(3) * down(c, 0))
            return out + (co(4) * up(c, 1) + co(5) * down(c, 1))

        def main_sweep(step, planes):
            read, write = (SA, SB) if step % 2 == 0 else (SB, SA)
            for p in planes:
                write[p] = jacobi(lambda m: CO[m, p], read[p], read[p + 1], read[p - 1])

        inner = [range(HALO + 1 + t, HALO + nx - 1 - t) for t in range(SWEEPS)]
        lax.fori_loop(HALO, HALO + nx, velocities, 0, unroll=4)
        lax.fori_loop(inner[0].start, inner[0].stop, coefficients, 0, unroll=3)
        for step in range(SWEEPS):
            main_sweep(step, inner[step])

        for side in (0, 1):
            for c in x_copies[side]:
                c.wait_recv()
            for c in relays[side]:
                c.start()
        for (dz, j), both in pack_relays.items():
            for c in packs[(0, dz, j)]:
                c.wait_recv()
            for c in both:
                c.start()
        for side in (0, 1):
            base = 0 if side == 0 else HALO + nx
            ebase = HALO - REACH if side == 0 else HALO + nx
            for k in range(HALO):
                for f in range(4):
                    QF[f, base + k, own_y] = xq[sec, side, f, k].astype(F32)
                SA[base + k, own_y] = xs[sec, side, k].astype(F32)
            for k in range(REACH):
                QF[4, ebase + k, own_y] = xe[sec, side, k].astype(F32)

        def x_face(p):
            left, right = [], []
            for f in range(5):
                v = [QF[f, p + o, own_y] for o in range(-2, 4)]
                left.append(edges(v[2], v[3], v[1], v[4], v[0])[0])
                right.append(edges(v[3], v[4], v[2], v[5], v[1])[1])
            return face_flux(left, right, 0)

        def x_flux(k, before):
            h = x_face(HALO + k)
            for f in range(5):
                T[f, k] = T[f, k] + (h[f] - before[f])
            return tuple(h)

        lax.fori_loop(0, nx, x_flux, tuple(x_face(HALO - 1)), unroll=4)

        windows(0, 0, 4)
        windows(2, 0, 4)
        for side in (0, 1):
            base = 0 if side == 0 else HALO + nx
            for c in relays[side]:
                c.wait_recv()
            for k in range(HALO):
                for f in range(4):
                    QF[f, base + k, far_y] = yxq[sec, side, f, k].astype(F32)
                SA[base + k, far_y] = yxs[sec, side, k].astype(F32)
        for both in pack_relays.values():
            for c in both:
                c.wait_recv()
        windows(0, 1, 4)
        windows(2, 1, 4)

        for base in (0, HALO + nx):
            for p in range(base, base + HALO):
                velocities(p, 0)
        for n in range(6):
            inv = 1.0 / WQ[0, n]
            WI[n] = inv
            for a in range(3):
                WU[a, n] = WQ[1 + a, n] * inv

        for p in range(1, px - 1):
            if p not in inner[0]:
                coefficients(p, 0)

        def in_x(ref, n):
            v = ref[n]
            after = ref[n + 2] if n < 4 else None
            before = ref[n - 2] if n > 1 else None
            return x_next(v, n, after), x_prev(v, n, before)

        for n in range(6):
            g = []
            for a in range(3):
                u = WU[a, n]
                hi_x, lo_x = in_x(WU.at[a], n)
                g.append([hi_x - lo_x, up(u, 0) - down(u, 0), up(u, 1) - down(u, 1)])
            c = WI[n]
            around = list(in_x(WI, n)) + [up(c, 0), down(c, 0), up(c, 1), down(c, 1)]
            for m, v in enumerate(stencil_terms(g, c, around)):
                WC[m, n] = v

        wread, wwrite = WA, WB
        for step in range(SWEEPS):
            main_sweep(step, [p for p in range(step + 1, px - 1 - step) if p not in inner[step]])
            for n in range(6):
                xp, xm = in_x(wread, n)
                wwrite[n] = jacobi(lambda m: WC[m, n], wread[n], xp, xm)
            wread, wwrite = wwrite, wread
        S, WS = (SA if SWEEPS % 2 == 0 else SB), wread

        edge = jnp.logical_or(lane2 < SWEEPS, lane2 >= nz - SWEEPS)
        joined = [jnp.where(lower2, WS[2 * g + 1], WS[2 * g]) for g in range(3)]
        for k in range(-1, nx + 1):
            p = HALO + k
            g, at = (k + nx) // nx, (k + nx) % nx
            S[p] = jnp.where(edge, pltpu.roll(joined[g], nz - half - slot * at, 1), S[p])
        diffs = []
        for n in (2, 3):
            v = WS[n, own_y]
            e = v * WU[2, n, own_y]
            diffs.append((up(v, 1) - down(v, 1), up(e, 1) - down(e, 1)))
        for i in (0, 1):
            ZB[i] = jnp.where(lower, diffs[1][i], diffs[0][i])
        ends = jnp.logical_or(lane == 0, lane == nz - 1)

        def finish(k, carry):
            p = HALO + k
            shift = nz - half - slot * k
            push = [T[f, k] for f in range(5)]
            xp, xm = S[p + 1, own_y], S[p - 1, own_y]
            push[1] = push[1] + 0.5 * (xp - xm)
            power = xp * U[0, p + 1, own_y] - xm * U[0, p - 1, own_y]
            sy = S[p]
            push[2] = push[2] + 0.5 * (up(sy, 0) - down(sy, 0))[own_y]
            e = sy * U[1, p]
            power = power + (up(e, 0) - down(e, 0))[own_y]
            sz = S[p, own_y]
            dz = jnp.where(ends, pltpu.roll(ZB[0], shift, 1), up(sz, 1) - down(sz, 1))
            push[3] = push[3] + 0.5 * dz
            e = sz * U[2, p, own_y]
            power = power + jnp.where(ends, pltpu.roll(ZB[1], shift, 1), up(e, 1) - down(e, 1))
            push[4] = push[4] + 0.5 * power
            for f in range(5):
                initial = cons[f, k].astype(F32)
                moved = initial - time_step * push[f]
                new_out[f, k] = 0.5 * (moved + q[f, k].astype(F32))
                stq[sec + 1, f, k] = moved.astype(BF16)
            ent_out[k] = sz
            sts[sec + 1, k] = sz
            stb[sec + 1, k] = sz.astype(BF16)
            return carry

        lax.fori_loop(0, nx, finish, 0, unroll=4)
        for c in everything:
            c.wait_send()
        return carry

    stq[0] = cons[...]
    sts[0] = sigma[...]
    stb[0] = sigma[...].astype(BF16)
    barrier = pltpu.get_barrier_semaphore()
    for peer in peers:
        pl.semaphore_signal(barrier, inc=1, device_id=dev(*peer), device_id_type=MESH)
    pl.semaphore_wait(barrier, len(peers))
    lax.fori_loop(0, 2, section, 0)


def slot_ok(nz, nx):
    return nz % nx == 0 and (nz // nx) & (nz // nx - 1) == 0


def solution(mesh):
    counts = (mesh.shape["gx"], mesh.shape["gy"], mesh.shape["gz"])
    assert counts[1] == 2 and counts[2] == 2

    def step(conserved, sigma_prev):
        _, nx, ny, nz = conserved.shape
        px = nx + 2 * HALO
        wide = (2 * ny, nz)
        assert nx >= HALO and nz // nx >= 4 * SWEEPS and slot_ok(nz, nx)
        vmem = pl.BlockSpec(memory_space=pltpu.VMEM)
        return pl.pallas_call(
            functools.partial(kernel, counts),
            out_shape=(
                pltpu.VMEM((5, nx, ny, nz), F32),
                pltpu.VMEM((nx, ny, nz), F32),
            ),
            in_specs=[vmem, vmem],
            out_specs=(vmem, vmem),
            scratch_shapes=[
                pltpu.VMEM((2, 2, 4, HALO, ny, nz), BF16),
                pltpu.VMEM((2, 2, REACH, ny, nz), BF16),
                pltpu.VMEM((2, 2, HALO, ny, nz), BF16),
                pltpu.VMEM((2, 5, nx, ny, nz), BF16),
                pltpu.VMEM((2, nx, ny, nz), F32),
                pltpu.VMEM((2, 2, 4, HALO, ny, nz), BF16),
                pltpu.VMEM((2, 2, HALO, ny, nz), BF16),
                pltpu.VMEM((2, 5, ny, nz), BF16),
                pltpu.VMEM((2, ny, nz), F32),
                pltpu.VMEM((2, 2, 2, 3, 5, ny, nz), BF16),
                pltpu.VMEM((2, 2, 2, 3, ny, nz), F32),
                pltpu.VMEM((3, 5, nx, ny, nz), BF16),
                pltpu.VMEM((3, nx, ny, nz), F32),
                pltpu.VMEM((3, nx, ny, nz), BF16),
                pltpu.VMEM((5, px) + wide, F32),
                pltpu.VMEM((3, px) + wide, F32),
                pltpu.VMEM((px,) + wide, F32),
                pltpu.VMEM((7, px) + wide, F32),
                pltpu.VMEM((px,) + wide, F32),
                pltpu.VMEM((px,) + wide, F32),
                pltpu.VMEM((5, 6) + wide, F32),
                pltpu.VMEM((3, 6) + wide, F32),
                pltpu.VMEM((6,) + wide, F32),
                pltpu.VMEM((7, 6) + wide, F32),
                pltpu.VMEM((6,) + wide, F32),
                pltpu.VMEM((6,) + wide, F32),
                pltpu.VMEM((5, ny, nz), F32),
                pltpu.VMEM((5, nx, ny, nz), F32),
                pltpu.SemaphoreType.DMA((2, 34)),
                pltpu.SemaphoreType.DMA((2, 34)),
            ],
            compiler_params=pltpu.CompilerParams(collective_id=0, has_side_effects=True),
        )(conserved, sigma_prev)

    return jax.shard_map(
        step,
        mesh=mesh,
        in_specs=(P(None, "gx", "gy", "gz"), P("gx", "gy", "gz")),
        out_specs=(P(None, "gx", "gy", "gz"), P("gx", "gy", "gz")),
        check_vma=False,
    )
```

```python
import functools

import jax
import jax.numpy as jnp
from jax import lax
from jax.experimental import pallas as pl
from jax.experimental.pallas import tpu as pltpu
from jax.sharding import PartitionSpec as P

SWEEPS = 4
HALO = SWEEPS + 1
REACH = 3
gamma_gas = 1.4
alpha_reg = 4.0
time_step = 0.08
MESH = pl.DeviceIdType.MESH
F32 = jnp.float32
BF16 = jnp.bfloat16


def edges(c, p1, m1, p2, m2):
    even = (47.0 / 60.0) * c + (7.0 / 60.0) * (p1 + m1) - (0.5 / 60.0) * (p2 + m2)
    odd = (20.0 / 60.0) * (p1 - m1) - (2.5 / 60.0) * (p2 - m2)
    return even + odd, even - odd


def physical_flux(v, d):
    inv = 1.0 / v[0]
    u = [v[1] * inv, v[2] * inv, v[3] * inv]
    kinetic = 0.5 * (v[1] * u[0] + v[2] * u[1] + v[3] * u[2])
    p = (gamma_gas - 1.0) * (v[4] - kinetic)
    n = u[d]
    flux = [v[1 + d], v[1] * n, v[2] * n, v[3] * n, (v[4] + p) * n]
    flux[1 + d] = flux[1 + d] + p
    return flux, jnp.abs(n) + jnp.sqrt(gamma_gas * jnp.abs(p) * inv)


def face_flux(left, right, d):
    fl, sl = physical_flux(left, d)
    fr, sr = physical_flux(right, d)
    speed = jnp.maximum(sl, sr)
    return [0.5 * ((a + b) - speed * (r - l)) for a, b, l, r in zip(fl, fr, left, right)]


def up(v, axis, by=1):
    return pltpu.roll(v, (v.shape[axis] - by) % v.shape[axis], axis)


def down(v, axis, by=1):
    return pltpu.roll(v, by, axis)


def kernel(counts, cons, sigma, new_out, ent_out, xq, xe, xs, yq, ys, yxq, yxs, pq, ps, rq, rs,
           stq, sts, stb, QF, U, INV, CO, SA, SB, WQ, WU, WI, WC, WA, WB, ZB, T, send_sem, recv_sem):
    gx, gy, gz = lax.axis_index("gx"), lax.axis_index("gy"), lax.axis_index("gz")
    nx, ny, nz = sigma.shape
    px = nx + 2 * HALO
    slot = nz // nx
    half = slot // 2
    own_y, far_y = slice(0, ny), slice(ny, 2 * ny)

    def dev(dx, dy, dz):
        return (
            lax.rem(gx + dx + counts[0], counts[0]),
            lax.rem(gy + dy, counts[1]),
            lax.rem(gz + dz, counts[2]),
        )

    lane = lax.broadcasted_iota(jnp.int32, (ny, nz), 1)
    lane2 = lax.broadcasted_iota(jnp.int32, (2 * ny, nz), 1)
    lower = (lane & (slot - 1)) < half
    lower2 = (lane2 & (slot - 1)) < half

    def pack(sec, q, s):
        for f in range(6):
            acc = None
            for k in range(nx):
                v = q[f, k].astype(F32) if f < 5 else s[k]
                r = pltpu.roll(v, (half + slot * k) % nz, 1)
                acc = r if acc is None else jnp.where(lane >= slot * k, r, acc)
            if f < 5:
                pq[sec, f] = acc.astype(BF16)
            else:
                ps[sec] = acc

    peers = [(-1, 0, 0), (1, 0, 0), (0, 1, 0), (0, 0, 1), (0, 1, 1), (-1, 0, 1), (1, 0, 1)]

    def x_next(v, g, after):
        r = up(v, 1, slot)
        return r if after is None else jnp.where(lane2 >= nz - slot, up(after, 1, slot), r)

    def x_prev(v, g, before):
        r = down(v, 1, slot)
        return r if before is None else jnp.where(lane2 < slot, down(before, 1, slot), r)

    def section(sec, carry):
        q, s = stq.at[sec], sts.at[sec]
        number = [0]
        everything = []

        def copy(src, dst, where):
            k = number[0]
            number[0] += 1
            c = pltpu.make_async_remote_copy(
                src_ref=src, dst_ref=dst, send_sem=send_sem.at[sec, k],
                recv_sem=recv_sem.at[sec, k], device_id=dev(*where), device_id_type=MESH,
            )
            everything.append(c)
            return c

        x_copies = []
        for side in (0, 1):
            to = (1, 0, 0) if side == 0 else (-1, 0, 0)
            a = nx - HALO if side == 0 else 0
            b = nx - REACH if side == 0 else 0
            x_copies.append([
                copy(q.at[0:4, a:a + HALO], xq.at[sec, side], to),
                copy(stb.at[sec, a:a + HALO], xs.at[sec, side], to),
                copy(q.at[4, b:b + REACH], xe.at[sec, side], to),
            ])
        y_copies = [copy(q, yq.at[sec], (0, 1, 0)), copy(s, ys.at[sec], (0, 1, 0))]
        relays = [
            [copy(xq.at[sec, side], yxq.at[sec, side], (0, 1, 0)),
             copy(xs.at[sec, side], yxs.at[sec, side], (0, 1, 0))]
            for side in (0, 1)
        ]
        packs, pack_relays = {}, {}
        for dx, dy, dz in ((0, 0, 1), (0, 1, 0), (0, 1, 1)):
            packs[(dy, dz, 1)] = [
                copy(pq.at[sec], rq.at[sec, dy, dz, 1], (dx, dy, dz)),
                copy(ps.at[sec], rs.at[sec, dy, dz, 1], (dx, dy, dz)),
            ]
        for dz in (0, 1):
            for dx in (1, -1):
                j = 1 - dx
                packs[(0, dz, j)] = [
                    copy(pq.at[sec, 0:4], rq.at[sec, 0, dz, j, 0:4], (dx, 0, dz)),
                    copy(ps.at[sec], rs.at[sec, 0, dz, j], (dx, 0, dz)),
                ]
                pack_relays[(dz, j)] = [
                    copy(rq.at[sec, 0, dz, j, 0:4], rq.at[sec, 1, dz, j, 0:4], (0, 1, 0)),
                    copy(rs.at[sec, 0, dz, j], rs.at[sec, 1, dz, j], (0, 1, 0)),
                ]

        for pair in x_copies:
            for c in pair:
                c.start()
        for c in y_copies:
            c.start()
        pack(sec, q, s)
        for both in packs.values():
            for c in both:
                c.start()

        for k in range(nx):
            for f in range(5):
                QF[f, HALO + k, own_y] = q[f, k].astype(F32)
            SA[HALO + k, own_y] = s[k]

        def windows(g, dy, fields):
            rows = far_y if dy else own_y
            for f in range(fields + 1):
                if f < fields:
                    own = pq[sec, f] if (g, dy) == (1, 0) else rq[sec, dy, 0, g, f]
                    own, far = own.astype(F32), rq[sec, dy, 1, g, f].astype(F32)
                    WQ[f, 2 * g, rows] = jnp.where(lower, far, own)
                    WQ[f, 2 * g + 1, rows] = jnp.where(lower, own, far)
                else:
                    own = ps[sec] if (g, dy) == (1, 0) else rs[sec, dy, 0, g]
                    far = rs[sec, dy, 1, g]
                    WA[2 * g, rows] = jnp.where(lower, far, own)
                    WA[2 * g + 1, rows] = jnp.where(lower, own, far)

        for c in y_copies:
            c.wait_recv()
        for k in range(nx):
            for f in range(5):
                QF[f, HALO + k, far_y] = yq[sec, f, k].astype(F32)
            SA[HALO + k, far_y] = ys[sec, k]
        for which in ((0, 1, 1), (1, 0, 1), (1, 1, 1)):
            for c in packs[which]:
                c.wait_recv()
        windows(1, 0, 5)
        windows(1, 1, 4)

        def line_flux(fields, d, axis):
            left, right = [], []
            for c in fields:
                l, r = edges(c, up(c, axis), down(c, axis), up(c, axis, 2), down(c, axis, 2))
                left.append(l)
                right.append(up(r, axis))
            return [v - down(v, axis) for v in face_flux(left, right, d)]

        lo = line_flux([WQ[f, 2, own_y] for f in range(5)], 2, 1)
        hi = line_flux([WQ[f, 3, own_y] for f in range(5)], 2, 1)
        for f in range(5):
            ZB[f] = jnp.where(lower, hi[f], lo[f])

        near = jnp.logical_or(lane < REACH, lane >= nz - REACH)

        def side_flux(k, carry):
            p = HALO + k
            ychange = line_flux([QF[f, p] for f in range(5)], 1, 0)
            zchange = line_flux([QF[f, p, own_y] for f in range(5)], 2, 1)
            shift = nz - half - slot * k
            for f in range(5):
                z = jnp.where(near, pltpu.roll(ZB[f], shift, 1), zchange[f])
                T[f, k] = ychange[f][own_y] + z
            return carry

        lax.fori_loop(0, nx, side_flux, 0, unroll=4)

        def velocities(p, carry):
            inv = 1.0 / QF[0, p]
            INV[p] = inv
            for a in range(3):
                U[a, p] = QF[1 + a, p] * inv
            return carry

        def stencil_terms(g, c, around):
            div = g[0][0] + g[1][1] + g[2][2]
            total = div * div + g[0][0] * g[0][0] + g[1][1] * g[1][1] + g[2][2] * g[2][2]
            total = total + 2.0 * (g[0][1] * g[1][0] + g[0][2] * g[2][0] + g[1][2] * g[2][1])
            source = (alpha_reg * 0.25) * total
            w = [(alpha_reg * 0.5) * (c + n) for n in around]
            scale = 1.0 / (c + ((w[0] + w[1]) + (w[2] + w[3]) + (w[4] + w[5])))
            return [v * scale for v in w] + [source * scale]

        def coefficients(p, carry):
            g = []
            for a in range(3):
                u = U[a, p]
                g.append([
                    U[a, p + 1] - U[a, p - 1], up(u, 0) - down(u, 0), up(u, 1) - down(u, 1),
                ])
            c = INV[p]
            around = [INV[p + 1], INV[p - 1], up(c, 0), down(c, 0), up(c, 1), down(c, 1)]
            for n, v in enumerate(stencil_terms(g, c, around)):
                CO[n, p] = v
            return carry

        def jacobi(co, c, xp, xm):
            out = co(6) + co(0) * xp + co(1) * xm
            out = out + (co(2) * up(c, 0) + co(3) * down(c, 0))
            return out + (co(4) * up(c, 1) + co(5) * down(c, 1))

        def main_sweep(step, planes):
            read, write = (SA, SB) if step % 2 == 0 else (SB, SA)
            for p in planes:
                write[p] = jacobi(lambda m: CO[m, p], read[p], read[p + 1], read[p - 1])

        inner = [range(HALO + 1 + t, HALO + nx - 1 - t) for t in range(SWEEPS)]
        lax.fori_loop(HALO, HALO + nx, velocities, 0, unroll=4)
        lax.fori_loop(inner[0].start, inner[0].stop, coefficients, 0, unroll=3)
        for step in range(SWEEPS):
            main_sweep(step, inner[step])

        for side in (0, 1):
            for c in x_copies[side]:
                c.wait_recv()
            for c in relays[side]:
                c.start()
        for (dz, j), both in pack_relays.items():
            for c in packs[(0, dz, j)]:
                c.wait_recv()
            for c in both:
                c.start()
        for side in (0, 1):
            base = 0 if side == 0 else HALO + nx
            ebase = HALO - REACH if side == 0 else HALO + nx
            for k in range(HALO):
                for f in range(4):
                    QF[f, base + k, own_y] = xq[sec, side, f, k].astype(F32)
                SA[base + k, own_y] = xs[sec, side, k].astype(F32)
            for k in range(REACH):
                QF[4, ebase + k, own_y] = xe[sec, side, k].astype(F32)

        def x_face(p):
            left, right = [], []
            for f in range(5):
                v = [QF[f, p + o, own_y] for o in range(-2, 4)]
                left.append(edges(v[2], v[3], v[1], v[4], v[0])[0])
                right.append(edges(v[3], v[4], v[2], v[5], v[1])[1])
            return face_flux(left, right, 0)

        def x_flux(k, before):
            h = x_face(HALO + k)
            for f in range(5):
                T[f, k] = T[f, k] + (h[f] - before[f])
            return tuple(h)

        lax.fori_loop(0, nx, x_flux, tuple(x_face(HALO - 1)), unroll=4)

        windows(0, 0, 4)
        windows(2, 0, 4)
        for side in (0, 1):
            base = 0 if side == 0 else HALO + nx
            for c in relays[side]:
                c.wait_recv()
            for k in range(HALO):
                for f in range(4):
                    QF[f, base + k, far_y] = yxq[sec, side, f, k].astype(F32)
                SA[base + k, far_y] = yxs[sec, side, k].astype(F32)
        for both in pack_relays.values():
            for c in both:
                c.wait_recv()
        windows(0, 1, 4)
        windows(2, 1, 4)

        for base in (0, HALO + nx):
            for p in range(base, base + HALO):
                velocities(p, 0)
        for n in range(6):
            inv = 1.0 / WQ[0, n]
            WI[n] = inv
            for a in range(3):
                WU[a, n] = WQ[1 + a, n] * inv

        for p in range(1, px - 1):
            if p not in inner[0]:
                coefficients(p, 0)

        def in_x(ref, n):
            v = ref[n]
            after = ref[n + 2] if n < 4 else None
            before = ref[n - 2] if n > 1 else None
            return x_next(v, n, after), x_prev(v, n, before)

        for n in range(6):
            g = []
            for a in range(3):
                u = WU[a, n]
                hi_x, lo_x = in_x(WU.at[a], n)
                g.append([hi_x - lo_x, up(u, 0) - down(u, 0), up(u, 1) - down(u, 1)])
            c = WI[n]
            around = list(in_x(WI, n)) + [up(c, 0), down(c, 0), up(c, 1), down(c, 1)]
            for m, v in enumerate(stencil_terms(g, c, around)):
                WC[m, n] = v

        wread, wwrite = WA, WB
        for step in range(SWEEPS):
            main_sweep(step, [p for p in range(step + 1, px - 1 - step) if p not in inner[step]])
            for n in range(6):
                xp, xm = in_x(wread, n)
                wwrite[n] = jacobi(lambda m: WC[m, n], wread[n], xp, xm)
            wread, wwrite = wwrite, wread
        S, WS = (SA if SWEEPS % 2 == 0 else SB), wread

        edge = jnp.logical_or(lane2 < SWEEPS, lane2 >= nz - SWEEPS)
        joined = [jnp.where(lower2, WS[2 * g + 1], WS[2 * g]) for g in range(3)]
        for k in range(-1, nx + 1):
            p = HALO + k
            g, at = (k + nx) // nx, (k + nx) % nx
            S[p] = jnp.where(edge, pltpu.roll(joined[g], nz - half - slot * at, 1), S[p])
        diffs = []
        for n in (2, 3):
            v = WS[n, own_y]
            e = v * WU[2, n, own_y]
            diffs.append((up(v, 1) - down(v, 1), up(e, 1) - down(e, 1)))
        for i in (0, 1):
            ZB[i] = jnp.where(lower, diffs[1][i], diffs[0][i])
        ends = jnp.logical_or(lane == 0, lane == nz - 1)

        def finish(k, carry):
            p = HALO + k
            shift = nz - half - slot * k
            push = [T[f, k] for f in range(5)]
            xp, xm = S[p + 1, own_y], S[p - 1, own_y]
            push[1] = push[1] + 0.5 * (xp - xm)
            power = xp * U[0, p + 1, own_y] - xm * U[0, p - 1, own_y]
            sy = S[p]
            push[2] = push[2] + 0.5 * (up(sy, 0) - down(sy, 0))[own_y]
            e = sy * U[1, p]
            power = power + (up(e, 0) - down(e, 0))[own_y]
            sz = S[p, own_y]
            dz = jnp.where(ends, pltpu.roll(ZB[0], shift, 1), up(sz, 1) - down(sz, 1))
            push[3] = push[3] + 0.5 * dz
            e = sz * U[2, p, own_y]
            power = power + jnp.where(ends, pltpu.roll(ZB[1], shift, 1), up(e, 1) - down(e, 1))
            push[4] = push[4] + 0.5 * power
            for f in range(5):
                initial = cons[f, k].astype(F32)
                moved = initial - time_step * push[f]
                new_out[f, k] = 0.5 * (moved + q[f, k].astype(F32))
                stq[sec + 1, f, k] = moved.astype(BF16)
            ent_out[k] = sz
            sts[sec + 1, k] = sz
            stb[sec + 1, k] = sz.astype(BF16)
            return carry

        lax.fori_loop(0, nx, finish, 0, unroll=nx)
        for c in everything:
            c.wait_send()
        return carry

    stq[0] = cons[...]
    sts[0] = sigma[...]
    stb[0] = sigma[...].astype(BF16)
    barrier = pltpu.get_barrier_semaphore()
    for peer in peers:
        pl.semaphore_signal(barrier, inc=1, device_id=dev(*peer), device_id_type=MESH)
    pl.semaphore_wait(barrier, len(peers))
    lax.fori_loop(0, 2, section, 0)


def slot_ok(nz, nx):
    return nz % nx == 0 and (nz // nx) & (nz // nx - 1) == 0


def solution(mesh):
    counts = (mesh.shape["gx"], mesh.shape["gy"], mesh.shape["gz"])
    assert counts[1] == 2 and counts[2] == 2

    def step(conserved, sigma_prev):
        _, nx, ny, nz = conserved.shape
        px = nx + 2 * HALO
        wide = (2 * ny, nz)
        assert nx >= HALO and nz // nx >= 4 * SWEEPS and slot_ok(nz, nx)
        vmem = pl.BlockSpec(memory_space=pltpu.VMEM)
        return pl.pallas_call(
            functools.partial(kernel, counts),
            out_shape=(
                pltpu.VMEM((5, nx, ny, nz), F32),
                pltpu.VMEM((nx, ny, nz), F32),
            ),
            in_specs=[vmem, vmem],
            out_specs=(vmem, vmem),
            scratch_shapes=[
                pltpu.VMEM((2, 2, 4, HALO, ny, nz), BF16),
                pltpu.VMEM((2, 2, REACH, ny, nz), BF16),
                pltpu.VMEM((2, 2, HALO, ny, nz), BF16),
                pltpu.VMEM((2, 5, nx, ny, nz), BF16),
                pltpu.VMEM((2, nx, ny, nz), F32),
                pltpu.VMEM((2, 2, 4, HALO, ny, nz), BF16),
                pltpu.VMEM((2, 2, HALO, ny, nz), BF16),
                pltpu.VMEM((2, 5, ny, nz), BF16),
                pltpu.VMEM((2, ny, nz), F32),
                pltpu.VMEM((2, 2, 2, 3, 5, ny, nz), BF16),
                pltpu.VMEM((2, 2, 2, 3, ny, nz), F32),
                pltpu.VMEM((3, 5, nx, ny, nz), BF16),
                pltpu.VMEM((3, nx, ny, nz), F32),
                pltpu.VMEM((3, nx, ny, nz), BF16),
                pltpu.VMEM((5, px) + wide, F32),
                pltpu.VMEM((3, px) + wide, F32),
                pltpu.VMEM((px,) + wide, F32),
                pltpu.VMEM((7, px) + wide, F32),
                pltpu.VMEM((px,) + wide, F32),
                pltpu.VMEM((px,) + wide, F32),
                pltpu.VMEM((5, 6) + wide, F32),
                pltpu.VMEM((3, 6) + wide, F32),
                pltpu.VMEM((6,) + wide, F32),
                pltpu.VMEM((7, 6) + wide, F32),
                pltpu.VMEM((6,) + wide, F32),
                pltpu.VMEM((6,) + wide, F32),
                pltpu.VMEM((5, ny, nz), F32),
                pltpu.VMEM((5, nx, ny, nz), F32),
                pltpu.SemaphoreType.DMA((2, 34)),
                pltpu.SemaphoreType.DMA((2, 34)),
            ],
            compiler_params=pltpu.CompilerParams(collective_id=0, has_side_effects=True),
        )(conserved, sigma_prev)

    return jax.shard_map(
        step,
        mesh=mesh,
        in_specs=(P(None, "gx", "gy", "gz"), P("gx", "gy", "gz")),
        out_specs=(P(None, "gx", "gy", "gz"), P("gx", "gy", "gz")),
        check_vma=False,
    )
```
